32 devices in a mesh: seq: 16 (over z, y, x), head: 2 (over core).
Axes of the slice: x: 2, y: 2, z: 4, core: 2. Of those that a mesh axis runs over, the one named last changes fastest.
Arguments:
- query_rows: bfloat16 [16384, 2048], P('seq', 'head'), may hold values from -6 to 6
- key_rows: bfloat16 [16384, 2048], P('seq', 'head'), may hold values from -6 to 6
- value_rows: bfloat16 [16384, 2048], P('seq', 'head'), may hold values from -16 to 16
- level_codes: int32 [16, 20, 16], P('seq', None, 'head'), may hold values from 1 to 8
- norm_gain: float32 [2048], P('head'), may hold values from 0.1 to 1.9
- upstream: bfloat16 [16384, 2048], P('seq', 'head'), may hold values from -6 to 6
Outputs:
- normed: bfloat16 [16384, 2048], P('seq', 'head')
- query_gradient: bfloat16 [16384, 2048], P('seq', 'head')
- key_gradient: bfloat16 [16384, 2048], P('seq', 'head')
- value_gradient: bfloat16 [16384, 2048], P('seq', 'head')
The draws below stay inside these ranges and needn't reach their ends.
All inputs are finite; a program needn't handle non-finite values.
Results may differ from the reference program's by a relative error of at most 0.0059.
Values sent between devices are 32-bit elements; how exact they have to be, the bound alone decides.
No kernel may reach another device: no remote copies, remote signals or barrier semaphores. Data moves between devices by JAX's collectives and lax.ppermute only.
A program may use at most 128 MiB of HBM per device.

```python
import jax
import jax.numpy as jnp
from jax import lax

HEADS = 16
DK = 128
DV = 128
GROUP = 1024
LEVELS = 20
SEQ = 16384
NCH = 16
FEAT = 2048


def draw_value_rows(key, part):
    columns = jnp.arange(HEADS * DV, dtype=jnp.int32) // DV
    fraction = columns.astype(jnp.float32) / (HEADS - 1)
    spread = 0.4 * jnp.power(10.0, fraction)
    sample = jnp.clip(jax.random.normal(key, (SEQ, HEADS * DV), jnp.float32), -4.0, 4.0)
    return (sample * spread[None, :]).astype(jnp.bfloat16)


def touch_ends(drawn, key, smallest, high):
    dims = drawn.shape
    spot = [jax.random.randint(jax.random.fold_in(key, axis), (), 0, dims[axis]) for axis in range(len(dims))]
    drawn = drawn.at[tuple(spot)].set(smallest)
    longest = dims.index(max(dims))
    spot[longest] = (spot[longest] + 1) % dims[longest]
    return drawn.at[tuple(spot)].set(high)


def block_levels(own_key, shape, shards, least, high):
    def one(axis_at, parts):
        steps = jax.random.uniform(jax.random.fold_in(jax.random.fold_in(own_key, 6), axis_at), (parts,), jnp.float32, least / len(shards), high / len(shards))
        return jnp.repeat(jnp.exp(steps), shape[axis_at] // parts).reshape((-1,) + (1,) * (len(shape) - axis_at - 1))

    level = one(*shards[0])
    for cut in shards[1:]:
        level = level * one(*cut)
    return level


def normal_values(rng, dims, deviation, reach, split=(), kind=jnp.bfloat16):
    result = deviation * jax.random.normal(rng, dims, jnp.float32)
    if split:
        result = result * block_levels(rng, dims, split, -0.22, 0.18)
    return jnp.clip(result, -reach, reach).astype(kind)


def setup_inputs(seed: int = 0) -> dict:
    seeds = jax.random.split(jax.random.key(seed), 7)
    return {
        "query_rows": normal_values(seeds[0], (SEQ, FEAT), 1.0, 6.0, ((0, 16), (1, 2))),
        "key_rows": normal_values(seeds[1], (SEQ, FEAT), 1.0, 6.0, ((0, 16), (1, 2))),
        "value_rows": draw_value_rows(jax.random.fold_in(seeds[6], 71), 0),
        "level_codes": touch_ends(jax.random.randint(seeds[3], (NCH, LEVELS, HEADS), 1, 9), jax.random.fold_in(seeds[3], 1), 1, 8).astype(jnp.int32),
        "norm_gain": jnp.clip(1.0 + 0.18 * jax.random.normal(seeds[4], (FEAT,), jnp.float32), 0.1, 1.9),
        "upstream": normal_values(seeds[5], (SEQ, FEAT), 1.0, 6.0, ((0, 16), (1, 2))),
    }


def level_scale(level_codes):
    levels_total = level_codes.shape[1]
    levels = jnp.arange(levels_total, dtype=jnp.float32)
    factor = jnp.where(levels > 0, jnp.exp2(-(levels - 1.0) * 0.5), 1.0) * 0.25
    return level_codes.astype(jnp.float32) * factor[None, :, None] * DK ** (-0.5)

def bit_length(number, places):
    running = jnp.zeros_like(number)
    for offset in range(places):
        running = running + (jnp.right_shift(number, offset) > 0).astype(jnp.int32)
    return running

def token_levels(extent, places):
    row_index = lax.broadcasted_iota(jnp.int32, (extent, extent), 0)
    column_index = lax.broadcasted_iota(jnp.int32, (extent, extent), 1)
    levels = bit_length(jnp.bitwise_xor(row_index, column_index), places)
    return jnp.where(column_index <= row_index, levels, -1)

def pair_weights(levels, level_rows, places):
    weights = jnp.zeros((level_rows.shape[0],) + levels.shape, jnp.float32)
    for which_level in range(places + 1):
        weights = jnp.where(levels[None] == which_level, level_rows[:, which_level][:, None, None], weights)
    return weights

def fenwick_map(states, head_levels, places):
    group_index = jnp.arange(NCH, dtype=jnp.int32)
    running_map = jnp.zeros_like(states)
    for which_bit in range((NCH - 1).bit_length()):
        block_sums = states.reshape(NCH >> which_bit, 1 << which_bit, states.shape[1], states.shape[2]).sum(axis=1)
        shifted = jnp.right_shift(group_index, which_bit)
        partner_block = jnp.bitwise_xor(shifted, 1)
        upper_half = shifted % 2 == 1
        factor = jnp.where(upper_half, head_levels[:, places + which_bit + 1], 0.0)
        running_map = running_map + factor[:, None, None] * block_sums[partner_block]
    return running_map

def fenwick_readers(map_grad, head_levels, places):
    group_index = jnp.arange(NCH, dtype=jnp.int32)
    received = jnp.zeros_like(map_grad)
    for which_bit in range((NCH - 1).bit_length()):
        shifted = jnp.right_shift(group_index, which_bit)
        partner_block = jnp.bitwise_xor(shifted, 1)
        upper_half = shifted % 2 == 1
        weighted = jnp.where(upper_half, head_levels[:, places + which_bit + 1], 0.0)[:, None, None] * map_grad
        block_sums = weighted.reshape(NCH >> which_bit, 1 << which_bit, map_grad.shape[1], map_grad.shape[2]).sum(axis=1)
        received = received + jnp.where(upper_half, 0.0, 1.0)[:, None, None] * block_sums[partner_block]
    return received

def head_tables(query_head, key_head, value_head, head_levels):
    places = GROUP.bit_length() - 1
    query_wide = query_head.astype(jnp.float32)
    key_wide = key_head.astype(jnp.float32)
    value_wide = value_head.astype(jnp.float32)
    scores = jnp.einsum('ctd,csd->cts', query_wide, key_wide, precision=lax.Precision.HIGHEST)
    weights = pair_weights(token_levels(GROUP, places), head_levels, places)
    attention = (weights * scores).astype(jnp.bfloat16)
    states = jnp.einsum('csd,cse->cde', key_wide, value_wide, precision=lax.Precision.HIGHEST)
    group_map = fenwick_map(states, head_levels, places).astype(jnp.bfloat16)
    return (weights, attention, group_map)

def head_forward(pieces):
    query_head, key_head, value_head, head_levels = pieces
    weights, attention, group_map = head_tables(query_head, key_head, value_head, head_levels)
    inside = jnp.einsum('cts,cse->cte', attention.astype(jnp.float32), value_head.astype(jnp.float32), precision=lax.Precision.HIGHEST)
    across = jnp.einsum('ctd,cde->cte', query_head.astype(jnp.float32), group_map.astype(jnp.float32), precision=lax.Precision.HIGHEST)
    return inside + across

def head_backward(pieces):
    query_head, key_head, value_head, head_levels, grad_head = pieces
    places = GROUP.bit_length() - 1
    weights, attention, group_map = head_tables(query_head, key_head, value_head, head_levels)
    query_wide = query_head.astype(jnp.float32)
    key_wide = key_head.astype(jnp.float32)
    value_wide = value_head.astype(jnp.float32)
    grad_wide = grad_head.astype(jnp.float32)
    pair_grad = jnp.einsum('cte,cse->cts', grad_wide, value_wide, precision=lax.Precision.HIGHEST)
    score_grad = (weights * pair_grad).astype(jnp.bfloat16).astype(jnp.float32)
    query_part = jnp.einsum('cts,csd->ctd', score_grad, key_wide, precision=lax.Precision.HIGHEST)
    query_part = query_part + jnp.einsum('cte,cde->ctd', grad_wide, group_map.astype(jnp.float32), precision=lax.Precision.HIGHEST)
    key_inside = jnp.einsum('cts,ctd->csd', score_grad, query_wide, precision=lax.Precision.HIGHEST)
    value_inside = jnp.einsum('cts,cte->cse', attention.astype(jnp.float32), grad_wide, precision=lax.Precision.HIGHEST)
    map_grad = jnp.einsum('ctd,cte->cde', query_wide, grad_wide, precision=lax.Precision.HIGHEST)
    state_grad = fenwick_readers(map_grad, head_levels, places).astype(jnp.bfloat16).astype(jnp.float32)
    key_part = key_inside + jnp.einsum('cse,cde->csd', value_wide, state_grad, precision=lax.Precision.HIGHEST)
    value_part = value_inside + jnp.einsum('csd,cde->cse', key_wide, state_grad, precision=lax.Precision.HIGHEST)
    return (query_part.astype(jnp.bfloat16), key_part.astype(jnp.bfloat16), value_part.astype(jnp.bfloat16))

def split_heads(matrix, width):
    return matrix.reshape(NCH, GROUP, HEADS, width).transpose(2, 0, 1, 3)

def merge_heads(stacked, width):
    return stacked.transpose(1, 2, 0, 3).reshape(SEQ, HEADS * width)

def reference(query_rows, key_rows, value_rows, level_codes, norm_gain, upstream):
    level_weights = level_scale(level_codes).transpose(2, 0, 1)
    query_split = split_heads(query_rows, DK)
    key_split = split_heads(key_rows, DK)
    value_split = split_heads(value_rows, DV)
    attended = merge_heads(lax.map(head_forward, (query_split, key_split, value_split, level_weights)), DV)
    row_squares = lax.optimization_barrier(jnp.sum(attended * attended, axis=1))
    inv_rms = lax.rsqrt(row_squares / (HEADS * DV) + 1e-06)
    normed = (attended * inv_rms[:, None] * norm_gain[None, :]).astype(jnp.bfloat16)
    scaled_grad = upstream.astype(jnp.float32) * norm_gain[None, :]
    row_dot = lax.optimization_barrier(jnp.sum(scaled_grad * attended, axis=1))
    attended_grad = (inv_rms[:, None] * scaled_grad - attended * (inv_rms ** 3 * row_dot / (HEADS * DV))[:, None]).astype(jnp.bfloat16)
    grad_split = split_heads(attended_grad, DV)
    query_part, key_part, value_part = lax.map(head_backward, (query_split, key_split, value_split, level_weights, grad_split))
    return (normed, merge_heads(query_part, DK), merge_heads(key_part, DK), merge_heads(value_part, DV))
```

```python
import functools
import math

import jax
import jax.numpy as jnp
from jax import lax
from jax.experimental import pallas as pl
from jax.experimental.pallas import tpu as pltpu
from jax.sharding import PartitionSpec as P

D = 128
GROUP = 1024
CHUNK = 128
ROWS = 256
F32 = jnp.float32
BF16 = jnp.bfloat16
VMEM_LIMIT = 40 << 20


def dot(a, b, ca, cb):
    return lax.dot_general(a, b, (((ca,), (cb,)), ((), ())), preferred_element_type=F32)


def level_scale(level_codes):
    levels = jnp.arange(level_codes.shape[1], dtype=F32)
    factor = jnp.where(levels > 0, jnp.exp2(-(levels - 1.0) * 0.5), 1.0) * 0.25
    return level_codes.astype(F32) * factor[None, :, None] * D ** (-0.5)


def log2(n):
    return n.bit_length() - 1


def tile_weights(lam, g, h, transposed=False):
    rows = lax.broadcasted_iota(jnp.int32, (CHUNK, CHUNK), 0)
    cols = lax.broadcasted_iota(jnp.int32, (CHUNK, CHUNK), 1)
    apart = rows ^ cols
    w = jnp.full((CHUNK, CHUNK), lam[g, 0, h], F32)
    for level in range(1, log2(CHUNK) + 1):
        w = jnp.where(apart >= (1 << (level - 1)), lam[g, level, h], w)
    return jnp.where(rows <= cols if transposed else rows >= cols, w, 0.0)


def chunk_maps(states, lam, h, reverse=False):
    count = len(states)
    per_group = GROUP // CHUNK
    first = log2(CHUNK) + 1
    maps = [None] * count

    def add(a, b):
        return b if a is None else a + b

    if not reverse:
        blocks = list(states)
        for bit in range(log2(count)):
            for i in range(count):
                if (i >> bit) & 1:
                    maps[i] = add(maps[i], lam[i // per_group, first + bit, h] * blocks[(i >> bit) ^ 1])
            blocks = [blocks[2 * a] + blocks[2 * a + 1] for a in range(len(blocks) // 2)]
    else:
        for bit in range(log2(count)):
            size = 1 << bit
            for block in range(1, count >> bit, 2):
                total = None
                for i in range(block * size, (block + 1) * size):
                    total = add(total, lam[i // per_group, first + bit, h] * states[i])
                for i in range((block - 1) * size, block * size):
                    maps[i] = add(maps[i], total)
    return maps


def state_kernel(heads_each, far, seg, pref, lam, k, v, *outs):
    m = pl.program_id(0)
    p = pref[0]
    part = m ^ p
    state = []
    for i in range(heads_each):
        state.append(dot(k[:, i * D : (i + 1) * D], v[:, i * D : (i + 1) * D], 0, 0))
    groups = lam.shape[0]
    first, bits = far
    for m_static, out in enumerate(outs):

        @pl.when(m == m_static)
        def _(out=out):
            for i in range(heads_each):
                out[i * D : (i + 1) * D, :] = state[i]
            row = heads_each * D
            for g in range(groups):
                for level in range(bits):
                    for i in range(heads_each):
                        out[row : row + 1, :] = jnp.full((1, D), lam[g, first + level, part * heads_each + i], F32)
                        row += 1
            while row < out.shape[0]:
                out[row : row + 1, :] = jnp.zeros((1, D), F32)
                row += 1


def inside_kernel(lam, q, k, v, part, maps_out):
    h = pl.program_id(0)
    count = q.shape[0] // CHUNK
    per_group = GROUP // CHUNK
    rows = [slice(i * CHUNK, (i + 1) * CHUNK) for i in range(count)]
    states = [dot(k[r, :], v[r, :], 0, 0) for r in rows]
    maps = chunk_maps(states, lam, h)
    for i, r in enumerate(rows):
        if i % per_group == 0:
            w = tile_weights(lam, i // per_group, h)
        a = (w * dot(q[r, :], k[r, :], 1, 1)).astype(BF16)
        if maps[i] is None:
            out = dot(a, v[r, :], 1, 0)
            maps_out[0, i] = jnp.zeros((D, D), BF16)
        else:
            m16 = maps[i].astype(BF16)
            maps_out[0, i] = m16
            out = dot(jnp.concatenate([a, q[r, :]], 1), jnp.concatenate([v[r, :], m16], 0), 1, 0)
        part[r, :] = out


def attend_kernel(pieces, heads_each, pref, q, part, u, gain, *refs):
    maps, (att, stats) = refs[:pieces], refs[pieces:]
    p = pref[0]
    g = (pl.program_id(0) * q.shape[0]) // GROUP
    squares = jnp.zeros((q.shape[0], D), F32)
    dots = jnp.zeros((q.shape[0], D), F32)
    for m in range(pieces):
        for i in range(heads_each):
            cols = pl.ds(pl.multiple_of(((m ^ p) * heads_each + i) * D, D), D)
            piece = maps[m][g, i * D : (i + 1) * D, :].astype(BF16)
            a = part[:, cols] + dot(q[:, cols], piece, 1, 0)
            att[:, cols] = a
            squares += a * a
            dots += (u[:, cols].astype(F32) * gain[:, cols]) * a
    stats[0:1, :] = jnp.sum(squares.T, axis=0, keepdims=True)
    stats[1:2, :] = jnp.sum(dots.T, axis=0, keepdims=True)


def grad_kernel(pieces, heads_each, features, pref, q, att, u, gain, stats, normed, grad, *map_grads):
    p = pref[0]
    step = pl.program_id(0)
    rows = q.shape[0]
    g = (step * rows) // GROUP
    inv = lax.rsqrt(stats[0:1, :] / features + 1e-06)
    beta = inv * inv * inv * stats[1:2, :] / features
    both = jnp.concatenate([inv, beta, jnp.zeros((6, rows), F32)], 0).T
    inv, beta = both[:, 0:1], both[:, 1:2]
    first = (step * rows) % GROUP == 0
    for m in range(pieces):
        for i in range(heads_each):
            cols = pl.ds(pl.multiple_of(((m ^ p) * heads_each + i) * D, D), D)
            a = att[:, cols]
            gn = gain[:, cols]
            normed[:, cols] = (a * inv * gn).astype(BF16)
            gr = (inv * (u[:, cols].astype(F32) * gn) - a * beta).astype(BF16)
            grad[:, cols] = gr
            mg = dot(q[:, cols], gr, 0, 0)
            where = (g, slice(i * D, (i + 1) * D), slice(None))

            @pl.when(first)
            def _(where=where, mg=mg, m=m):
                map_grads[m][where] = mg

            @pl.when(jnp.logical_not(first))
            def _(where=where, mg=mg, m=m):
                map_grads[m][where] += mg


def inner_grad_kernel(heads_each, pref, lam, q, k, v, grad, maps, far_map, dq, dk, dv):
    h = (pl.program_id(0) ^ pref[0]) * heads_each + pl.program_id(1)
    count = q.shape[0] // CHUNK
    per_group = GROUP // CHUNK
    rows = [slice(i * CHUNK, (i + 1) * CHUNK) for i in range(count)]
    map_grads = chunk_maps([dot(q[r, :], grad[r, :], 0, 0) for r in rows], lam, h, reverse=True)
    for i, r in enumerate(rows):
        group = i // per_group
        if i % per_group == 0:
            w = tile_weights(lam, group, h)
            wt = tile_weights(lam, group, h, transposed=True)
        at = (wt * dot(k[r, :], q[r, :], 1, 1)).astype(BF16)
        pg = (w * dot(grad[r, :], v[r, :], 1, 1)).astype(BF16)
        pt = (wt * dot(v[r, :], grad[r, :], 1, 1)).astype(BF16)
        reach = (maps[0, i].astype(F32) + far_map[0, group]).astype(BF16)
        dq[r, :] = (dot(pg, k[r, :], 1, 0) + dot(grad[r, :], reach, 1, 1)).astype(BF16)
        key = dot(pt, q[r, :], 1, 0)
        value = dot(at, grad[r, :], 1, 0)
        if map_grads[i] is not None:
            m16 = map_grads[i].astype(BF16)
            key = key + dot(v[r, :], m16, 1, 1)
            value = value + dot(k[r, :], m16, 1, 0)
        dk[r, :] = key
        dv[r, :] = value


def outer_grad_kernel(pieces, heads_each, pref, k, v, key_in, value_in, *refs):
    maps, (dk, dv) = refs[:pieces], refs[pieces:]
    p = pref[0]
    for m in range(pieces):
        for i in range(heads_each):
            cols = pl.ds(pl.multiple_of(((m ^ p) * heads_each + i) * D, D), D)
            piece = maps[m][i * D : (i + 1) * D, :].astype(BF16)
            dk[:, cols] = (key_in[:, cols] + dot(v[:, cols], piece, 1, 1)).astype(BF16)
            dv[:, cols] = (value_in[:, cols] + dot(k[:, cols], piece, 1, 0)).astype(BF16)


def exchange(x, axis, distance):
    count = lax.axis_size(axis)
    return lax.ppermute(x, axis, [(i, i ^ distance) for i in range(count)])


def sum_over(x, axis):
    count = lax.axis_size(axis)
    if count == 2:
        return x + exchange(x, axis, 1)
    return lax.psum(x, axis)


class Far:
    def __init__(self, groups, heads):
        self.count = lax.axis_size("seq")
        self.me = lax.axis_index("seq")
        self.inner = min(4, self.count)
        self.inner_bits = log2(self.inner)
        self.bits = log2(self.count)
        self.groups = groups
        self.rows = heads * D // self.inner
        self.seg = math.gcd(D, self.rows)
        self.segs = self.rows // self.seg
        used = groups * self.bits * self.segs
        self.extra = -(-used // 8) * 8
        self.p = self.me % self.inner
        self.outer = self.me // self.inner
        self.fast = self.rows % D == 0 and groups == 1

    def take(self, ext, m):
        used = self.groups * self.bits * self.segs
        return ext[m][:used].reshape(self.groups, self.bits, self.segs, 1, D)

    def forward(self, sends):
        got = [sends[0]] + [exchange(sends[m], "seq", m) for m in range(1, self.inner)]
        state = [x[: self.rows].reshape(self.segs, self.seg, D) for x in got]
        ext = [x[self.rows :] for x in got]
        total = functools.reduce(lambda a, b: a + b, state)
        outer = []
        for bit in range(self.bits - self.inner_bits):
            came = exchange(total.reshape(self.rows, D), "seq", self.inner << bit).reshape(total.shape)
            outer.append(came)
            total = total + came
        back = []
        for m in range(self.inner):
            w = self.take(ext, m)
            acc = jnp.zeros((self.groups, self.segs, self.seg, D), F32)
            for other in range(self.inner):
                if other != m:
                    reads = ((self.p ^ other) < (self.p ^ m)).astype(F32)
                    acc = acc + (w[:, (m ^ other).bit_length() - 1] * reads) * state[other][None]
            for bit, came in enumerate(outer):
                reads = ((self.outer >> bit) & 1).astype(F32)
                acc = acc + (w[:, self.inner_bits + bit] * reads) * came[None]
            back.append(acc.reshape(self.groups, self.rows, D))
        return [back[0]] + [exchange(back[m], "seq", m) for m in range(1, self.inner)], ext

    def backward(self, sends, ext):
        got = [sends[0]] + [exchange(sends[m], "seq", m) for m in range(1, self.inner)]
        grads = [x.reshape(self.groups, self.segs, self.seg, D) for x in got]
        weights = [self.take(ext, m) for m in range(self.inner)]

        def read_at(m, level):
            return jnp.sum(weights[m][:, level] * grads[m], axis=0)

        total = None
        for bit in reversed(range(self.bits - self.inner_bits)):
            reads = ((self.outer >> bit) & 1).astype(F32)
            send = reads * functools.reduce(
                lambda a, b: a + b, [read_at(m, self.inner_bits + bit) for m in range(self.inner)]
            )
            if total is not None:
                send = send + total
            came = exchange(send.reshape(self.rows, D), "seq", self.inner << bit).reshape(send.shape)
            total = came if total is None else total + came
        back = []
        for m in range(self.inner):
            acc = total if total is not None else jnp.zeros((self.segs, self.seg, D), F32)
            for other in range(self.inner):
                if other != m:
                    reads = ((self.p ^ other) > (self.p ^ m)).astype(F32)
                    acc = acc + reads * read_at(other, (m ^ other).bit_length() - 1)
            back.append(acc.reshape(self.rows, D))
        return [back[0]] + [exchange(back[m], "seq", m) for m in range(1, self.inner)]

    def gather_pieces(self, pieces):
        stacked = jnp.stack(pieces, 0)
        order = self.p ^ jnp.arange(self.inner)
        return jnp.moveaxis(jnp.take(stacked, order, axis=0), 0, -3).reshape(pieces[0].shape[:-2] + (self.inner * self.rows, D))

    def split_pieces(self, whole):
        parts = whole.reshape(whole.shape[:-2] + (self.inner, self.rows, D))
        return [lax.dynamic_index_in_dim(parts, self.p ^ m, parts.ndim - 3, keepdims=False) for m in range(self.inner)]


def local(query_rows, key_rows, value_rows, level_codes, norm_gain, upstream):
    tokens, width = query_rows.shape
    groups = tokens // GROUP
    heads = width // D
    features = width * lax.axis_size("head")
    chunks = tokens // CHUNK
    far = Far(groups, heads)
    first_far = log2(GROUP) + log2(groups) + 1
    lam = level_scale(level_codes)
    pieces, each = (far.inner, heads // far.inner) if far.fast else (1, heads)
    pref = (far.p if far.fast else jnp.zeros_like(far.p)).astype(jnp.int32).reshape(1)
    gain = norm_gain.reshape(1, width)
    steps = tokens // ROWS

    smem = pl.BlockSpec(memory_space=pltpu.SMEM)
    head_cols = pl.BlockSpec((tokens, D), lambda h: (0, h))
    row_block = pl.BlockSpec((ROWS, width), lambda i: (i, 0))
    row_stats = pl.BlockSpec((2, ROWS), lambda i: (0, i))
    whole_gain = pl.BlockSpec((1, width), lambda i: (0, 0))

    def params(**kw):
        return pltpu.CompilerParams(vmem_limit_bytes=VMEM_LIMIT, **kw)

    def cost(mults, moved):
        return pl.CostEstimate(flops=2 * mults, bytes_accessed=moved, transcendentals=0)

    unit = tokens * D * D * heads
    size = tokens * width * 2

    if far.fast:
        out_rows = far.rows + far.extra
        sends = pl.pallas_call(
            functools.partial(state_kernel, each, (first_far, far.bits), far.seg),
            grid_spec=pltpu.PrefetchScalarGridSpec(
                num_scalar_prefetch=1,
                grid=(far.inner,),
                in_specs=[smem] + [pl.BlockSpec((tokens, each * D), lambda m, pref: (0, m ^ pref[0]))] * 2,
                out_specs=[pl.BlockSpec((out_rows, D), lambda m, pref: (0, 0))] * far.inner,
            ),
            out_shape=[jax.ShapeDtypeStruct((out_rows, D), F32)] * far.inner,
            compiler_params=params(),
            cost_estimate=cost(unit, 2 * size),
            name="states",
        )(pref, lam, key_rows, value_rows)
    else:
        state = jnp.einsum(
            "she,shf->hef",
            key_rows.reshape(tokens, heads, D),
            value_rows.reshape(tokens, heads, D),
            preferred_element_type=F32,
        ).reshape(heads * D, D)
        per_row = jnp.repeat(lam[:, first_far : first_far + far.bits, :], D // far.seg, axis=2)
        sends = []
        for m, piece in enumerate(far.split_pieces(state)):
            w = lax.dynamic_slice_in_dim(per_row, (far.p ^ m) * far.segs, far.segs, 2).reshape(-1, 1)
            w = jnp.pad(w, ((0, far.extra - w.shape[0]), (0, 0)))
            sends.append(jnp.concatenate([piece, jnp.broadcast_to(w, (far.extra, D))], 0))

    part, maps = pl.pallas_call(
        inside_kernel,
        grid=(heads,),
        in_specs=[smem, head_cols, head_cols, head_cols],
        out_specs=[head_cols, pl.BlockSpec((1, chunks, D, D), lambda h: (h, 0, 0, 0))],
        out_shape=[
            jax.ShapeDtypeStruct((tokens, width), F32),
            jax.ShapeDtypeStruct((heads, chunks, D, D), BF16),
        ],
        compiler_params=params(),
        cost_estimate=cost(4 * unit, 6 * size),
        name="inside",
    )(lam, query_rows, key_rows, value_rows)

    far_maps, ext = far.forward(sends)
    if not far.fast:
        far_maps = [far.gather_pieces(far_maps)]
    piece_rows = each * D
    map_block = pl.BlockSpec((groups, piece_rows, D), lambda i: (0, 0, 0))

    att, stats = pl.pallas_call(
        functools.partial(attend_kernel, pieces, each),
        grid=(steps,),
        in_specs=[smem, row_block, row_block, row_block, whole_gain] + [map_block] * pieces,
        out_specs=[row_block, row_stats],
        out_shape=[jax.ShapeDtypeStruct((tokens, width), F32), jax.ShapeDtypeStruct((2, tokens), F32)],
        compiler_params=params(),
        cost_estimate=cost(unit, 6 * size),
        name="attend",
    )(pref, query_rows, part, upstream, gain, *far_maps)

    stats = sum_over(stats, "head")

    normed, grad, *map_grads = pl.pallas_call(
        functools.partial(grad_kernel, pieces, each, features),
        grid=(steps,),
        in_specs=[smem, row_block, row_block, row_block, whole_gain, row_stats],
        out_specs=[row_block, row_block] + [map_block] * pieces,
        out_shape=[
            jax.ShapeDtypeStruct((tokens, width), BF16),
            jax.ShapeDtypeStruct((tokens, width), BF16),
        ]
        + [jax.ShapeDtypeStruct((groups, piece_rows, D), F32)] * pieces,
        compiler_params=params(),
        cost_estimate=cost(unit, 6 * size),
        name="grads",
    )(pref, query_rows, att, upstream, gain, stats)

    if not far.fast:
        map_grads = far.split_pieces(map_grads[0])

    mh_cols = pl.BlockSpec((tokens, D), lambda m, i, pref: (0, (m ^ pref[0]) * each + i))
    far_stack = jnp.stack([f.reshape(groups, each, D, D) for f in far_maps], 0)
    far_stack = jnp.swapaxes(far_stack, 1, 2).reshape(pieces * each, groups, D, D)
    query_gradient, key_in, value_in = pl.pallas_call(
        functools.partial(inner_grad_kernel, each),
        grid_spec=pltpu.PrefetchScalarGridSpec(
            num_scalar_prefetch=1,
            grid=(pieces, each),
            in_specs=[smem]
            + [mh_cols] * 4
            + [
                pl.BlockSpec((1, chunks, D, D), lambda m, i, pref: ((m ^ pref[0]) * each + i, 0, 0, 0)),
                pl.BlockSpec((1, groups, D, D), lambda m, i, pref: (m * each + i, 0, 0, 0)),
            ],
            out_specs=[mh_cols] * 3,
        ),
        out_shape=[
            jax.ShapeDtypeStruct((tokens, width), BF16),
            jax.ShapeDtypeStruct((tokens, width), F32),
            jax.ShapeDtypeStruct((tokens, width), F32),
        ],
        compiler_params=params(),
        cost_estimate=cost(9 * unit, 9 * size),
        name="inner_grads",
    )(pref, lam, query_rows, key_rows, value_rows, grad, maps, far_stack)

    state_grads = far.backward(map_grads, ext)
    if not far.fast:
        state_grads = [far.gather_pieces(state_grads)]

    key_gradient, value_gradient = pl.pallas_call(
        functools.partial(outer_grad_kernel, pieces, each),
        grid=(steps,),
        in_specs=[smem] + [row_block] * 4 + [pl.BlockSpec((piece_rows, D), lambda i: (0, 0))] * pieces,
        out_specs=[row_block, row_block],
        out_shape=[jax.ShapeDtypeStruct((tokens, width), BF16)] * 2,
        compiler_params=params(),
        cost_estimate=cost(2 * unit, 8 * size),
        name="outer_grads",
    )(pref, key_rows, value_rows, key_in, value_in, *state_grads)
    return (normed, query_gradient, key_gradient, value_gradient)


def solution(mesh):
    return jax.shard_map(
        local,
        mesh=mesh,
        in_specs=(
            P("seq", "head"),
            P("seq", "head"),
            P("seq", "head"),
            P("seq", None, "head"),
            P("head"),
            P("seq", "head"),
        ),
        out_specs=(P("seq", "head"), P("seq", "head"), P("seq", "head"), P("seq", "head")),
        check_vma=False,
    )
```

```python
import functools
import math

import jax
import jax.numpy as jnp
from jax import lax
from jax.experimental import pallas as pl
from jax.experimental.pallas import tpu as pltpu
from jax.sharding import PartitionSpec as P


D = 128
GROUP = 1024
CHUNK = 128
F32 = jnp.float32
BF16 = jnp.bfloat16


def dot(a, b, ca, cb):
    return lax.dot_general(a, b, (((ca,), (cb,)), ((), ())), preferred_element_type=F32)


def level_scale(level_codes):
    levels = jnp.arange(level_codes.shape[1], dtype=F32)
    factor = jnp.where(levels > 0, jnp.exp2(-(levels - 1.0) * 0.5), 1.0) * 0.25
    return level_codes.astype(F32) * factor[None, :, None] * D ** (-0.5)


def log2(n):
    return n.bit_length() - 1


def weight(codes, g, level, h):
    factor = (2.0 ** (-(level - 1) / 2) if level else 1.0) / 4 / math.sqrt(D)
    return codes[g, level, h].astype(F32) * factor


def tile_weights(codes, g, h, transposed=False):
    rows = lax.broadcasted_iota(jnp.int32, (CHUNK, CHUNK), 0)
    cols = lax.broadcasted_iota(jnp.int32, (CHUNK, CHUNK), 1)
    apart = rows ^ cols
    w = jnp.full((CHUNK, CHUNK), weight(codes, g, 0, h), F32)
    for level in range(1, log2(CHUNK) + 1):
        w = jnp.where(apart >= (1 << (level - 1)), weight(codes, g, level, h), w)
    return jnp.where(rows <= cols if transposed else rows >= cols, w, 0.0)


def chunk_maps(states, codes, h, reverse=False):
    count = len(states)
    per_group = GROUP // CHUNK
    first = log2(CHUNK) + 1
    maps = [None] * count

    def add(a, b):
        return b if a is None else a + b

    if not reverse:
        blocks = list(states)
        for bit in range(log2(count)):
            for i in range(count):
                if (i >> bit) & 1:
                    maps[i] = add(maps[i], weight(codes, i // per_group, first + bit, h) * blocks[(i >> bit) ^ 1])
            blocks = [blocks[2 * a] + blocks[2 * a + 1] for a in range(len(blocks) // 2)]
    else:
        for bit in range(log2(count)):
            size = 1 << bit
            for block in range(1, count >> bit, 2):
                total = None
                for i in range(block * size, (block + 1) * size):
                    total = add(total, weight(codes, i // per_group, first + bit, h) * states[i])
                for i in range((block - 1) * size, block * size):
                    maps[i] = add(maps[i], total)
    return maps


def bf16_map(m):
    return jnp.zeros((D, D), BF16) if m is None else m.astype(BF16)


def chunk_rows(tokens):
    return [slice(i * CHUNK, (i + 1) * CHUNK) for i in range(tokens // CHUNK)]


def col(h):
    return pl.ds(pl.multiple_of(h * D, D), D)


def cat(a, b, axis):
    return jnp.concatenate([a, b], axis)


def state_kernel(parts, each, far, pref, codes, k_hbm, v_hbm, *refs):
    outs, (k, v, state, sems) = refs[:parts], refs[parts:]
    width = each * D
    copies = []
    for n in range(parts):
        cols = slice(n * width, (n + 1) * width)
        pair = [
            pltpu.make_async_copy(k_hbm.at[:, cols], k.at[n], sems.at[0, n]),
            pltpu.make_async_copy(v_hbm.at[:, cols], v.at[n], sems.at[1, n]),
        ]
        for c in pair:
            c.start()
        copies.append(pair)
    first, bits = far
    p = pref[0]
    for m, out in enumerate(outs):
        row = width
        for level in range(bits):
            for i in range(each):
                out[row : row + 1, :] = jnp.full((1, D), weight(codes, 0, first + level, (m ^ p) * each + i), F32)
                row += 1
        if row < out.shape[0]:
            out[row:, :] = jnp.zeros((out.shape[0] - row, D), F32)
    for n in range(parts):
        for c in copies[n]:
            c.wait()
        for i in range(each):
            cols = slice(i * D, (i + 1) * D)
            state[n, cols, :] = dot(k[n, :, cols], v[n, :, cols], 0, 0)
    for m, out in enumerate(outs):
        out[:width, :] = state[m ^ p]


def inside_kernel(pair, codes, q, k, v, part, maps, att_t, *tiles):
    rows = chunk_rows(q.shape[0])
    per_group = GROUP // CHUNK

    @pl.loop(0, q.shape[1] // D // pair)
    def _(step):
        heads = [step * pair + n for n in range(pair)]
        for n, h in enumerate(heads):
            c = col(h)
            for i, r in enumerate(rows):
                if i % per_group == 0:
                    w = tile_weights(codes, i // per_group, h)
                tiles[n][r, :] = (w * dot(q[r, c], k[r, c], 1, 1)).astype(BF16)
            for i, r in enumerate(rows):
                if i % per_group == 0:
                    w = tile_weights(codes, i // per_group, h, transposed=True)
                att_t[r, c] = (w * dot(k[r, c], q[r, c], 1, 1)).astype(BF16)
            reads = chunk_maps([dot(k[r, c], v[r, c], 0, 0) for r in rows], codes, h)
            for i in range(len(rows)):
                maps[h, i] = bf16_map(reads[i])
        for n, h in enumerate(heads):
            c = col(h)
            for i, r in enumerate(rows):
                part[r, c] = dot(cat(tiles[n][r, :], q[r, c], 1), cat(v[r, c], maps[h, i], 0), 1, 0)


def scale_kernel(u, gain, scaled):
    @pl.loop(0, u.shape[0] // CHUNK)
    def _(i):
        r = pl.ds(pl.multiple_of(i * CHUNK, CHUNK), CHUNK)
        scaled[r, :] = u[r, :].astype(F32) * gain[...]


def sort_pieces(pieces, each, p, out):
    for m, piece in enumerate(pieces):
        for g in range(piece.shape[0]):
            for i in range(each):
                out[(m ^ p) * each + i, g] = piece[g, i * D : (i + 1) * D, :].astype(out.dtype)


def attend_kernel(pieces, each, pref, q, part, scaled, *refs):
    far, (att, stats, maps) = refs[:pieces], refs[pieces:]
    sort_pieces(far, each, pref[0], maps)
    heads = q.shape[1] // D

    @pl.loop(0, q.shape[0] // CHUNK)
    def _(step):
        r = pl.ds(pl.multiple_of(step * CHUNK, CHUNK), CHUNK)
        g = (step * CHUNK) // GROUP
        squares = dots = None
        for h in range(heads):
            c = slice(h * D, (h + 1) * D)
            a = part[r, c] + dot(q[r, c], maps[h, g], 1, 0)
            att[r, c] = a
            squares = a * a if h == 0 else squares + a * a
            dots = scaled[r, c] * a if h == 0 else dots + scaled[r, c] * a
        stats[0:1, r] = jnp.sum(squares.T, axis=0, keepdims=True)
        stats[1:2, r] = jnp.sum(dots.T, axis=0, keepdims=True)


def token_factors(stats, features, inv_s, beta_s):
    @pl.loop(0, stats.shape[1] // CHUNK)
    def _(step):
        r = pl.ds(pl.multiple_of(step * CHUNK, CHUNK), CHUNK)
        inv = lax.rsqrt(stats[0:1, r] / features + 1e-06)
        inv_s[r, :] = jnp.broadcast_to(inv, (CHUNK, CHUNK)).T
        if beta_s is not None:
            beta = inv * inv * inv * stats[1:2, r] / features
            beta_s[r, :] = jnp.broadcast_to(beta, (CHUNK, CHUNK)).T


def grad_kernel(pieces, each, features, pref, q, att, scaled, stats, grad, *refs):
    outs, (inv, beta, sums) = refs[:pieces], refs[pieces:]
    token_factors(stats, features, inv, beta)
    groups = q.shape[0] // GROUP

    @pl.loop(0, q.shape[1] // D)
    def _(h):
        c = col(h)
        for r in chunk_rows(q.shape[0]):
            grad[r, c] = (inv[r, :] * scaled[r, c] - att[r, c] * beta[r, :]).astype(BF16)
        for g in range(groups):
            r = slice(g * GROUP, (g + 1) * GROUP)
            sums[h, g] = dot(q[r, c], grad[r, c], 0, 0)

    for m, out in enumerate(outs):
        for g in range(groups):
            for i in range(each):
                out[g, i * D : (i + 1) * D, :] = sums[(m ^ pref[0]) * each + i, g]


def query_kernel(pieces, each, features, pref, codes, k, v, grad, maps, att, stats, gain, *refs):
    far, (dq, normed, reach, inv, tiles, outer) = refs[:pieces], refs[pieces:]
    h = pl.program_id(0)

    @pl.when(h == 0)
    def _():
        token_factors(stats, features, inv, None)
        sort_pieces(far, each, pref[0], reach)

    c = col(h)
    rows = chunk_rows(k.shape[0])
    per_group = GROUP // CHUNK
    for i, r in enumerate(rows):
        if i % per_group == 0:
            w = tile_weights(codes, i // per_group, h)
        to = (maps[h, i].astype(F32) + reach[h, i // per_group]).astype(BF16)
        y = dot(grad[r, c], cat(v[r, c], to, 0), 1, 1)
        tiles[r, :] = (w * y[:, :D]).astype(BF16)
        outer[r, :] = y[:, D:]
    for r in rows:
        normed[r, :] = (att[r, c] * inv[r, :] * gain[:, c]).astype(BF16)
    for r in rows:
        dq[r, :] = (dot(tiles[r, :], k[r, c], 1, 0) + outer[r, :]).astype(BF16)


def key_kernel(codes, q, v, grad, key_in, readers, tiles, outer):
    rows = chunk_rows(q.shape[0])
    per_group = GROUP // CHUNK

    @pl.loop(0, q.shape[1] // D)
    def _(h):
        c = col(h)
        sums = chunk_maps([dot(q[r, c], grad[r, c], 0, 0) for r in rows], codes, h, reverse=True)
        for i in range(len(rows)):
            readers[h, i] = bf16_map(sums[i])
        for i, r in enumerate(rows):
            if i % per_group == 0:
                w = tile_weights(codes, i // per_group, h, transposed=True)
            y = dot(v[r, c], cat(grad[r, c], readers[h, i], 0), 1, 1)
            tiles[r, :] = (w * y[:, :D]).astype(BF16)
            outer[r, :] = y[:, D:]
        for r in rows:
            key_in[r, c] = dot(tiles[r, :], q[r, c], 1, 0) + outer[r, :]


def value_kernel(k, grad, att_t, readers, value_in):
    rows = chunk_rows(k.shape[0])

    @pl.loop(0, k.shape[1] // D)
    def _(h):
        c = col(h)
        for i, r in enumerate(rows):
            value_in[r, c] = dot(cat(att_t[r, c], k[r, c], 1), cat(grad[r, c], readers[h, i], 0), 1, 0)


def outer_kernel(pieces, each, pref, k, v, key_in, value_in, *refs):
    far, (dk, dv, maps) = refs[:pieces], refs[pieces:]
    step = pl.program_id(0)

    @pl.when(step == 0)
    def _():
        for m, piece in enumerate(far):
            for i in range(each):
                maps[(m ^ pref[0]) * each + i] = piece[i * D : (i + 1) * D, :].astype(BF16)

    r = pl.ds(pl.multiple_of(step * CHUNK, CHUNK), CHUNK)
    for h in range(k.shape[1] // D):
        c = slice(h * D, (h + 1) * D)
        dk[:, c] = (key_in[r, c] + dot(v[r, c], maps[h], 1, 1)).astype(BF16)
        dv[:, c] = (value_in[r, c] + dot(k[r, c], maps[h], 1, 0)).astype(BF16)


def exchange(x, axis, distance):
    count = lax.axis_size(axis)
    return lax.ppermute(x, axis, [(i, i ^ distance) for i in range(count)])


def sum_over(x, axis):
    count = lax.axis_size(axis)
    if count == 2:
        return x + exchange(x, axis, 1)
    return lax.psum(x, axis)


class Far:
    def __init__(self, groups, heads):
        self.count = lax.axis_size("seq")
        self.me = lax.axis_index("seq")
        self.inner = min(4, self.count)
        self.inner_bits = log2(self.inner)
        self.bits = log2(self.count)
        self.groups = groups
        self.rows = heads * D // self.inner
        self.seg = math.gcd(D, self.rows)
        self.segs = self.rows // self.seg
        used = groups * self.bits * self.segs
        self.extra = -(-used // 8) * 8
        self.p = self.me % self.inner
        self.outer = self.me // self.inner
        self.fast = self.rows % D == 0 and groups == 1

    def take(self, ext, m):
        used = self.groups * self.bits * self.segs
        return ext[m][:used].reshape(self.groups, self.bits, self.segs, 1, D)

    def forward(self, sends):
        got = [sends[0]] + [exchange(sends[m], "seq", m) for m in range(1, self.inner)]
        state = [x[: self.rows].reshape(self.segs, self.seg, D) for x in got]
        ext = [x[self.rows :] for x in got]
        total = functools.reduce(lambda a, b: a + b, state)
        outer = []
        for bit in range(self.bits - self.inner_bits):
            came = exchange(total.reshape(self.rows, D), "seq", self.inner << bit).reshape(total.shape)
            outer.append(came)
            total = total + came
        back = []
        for m in range(self.inner):
            w = self.take(ext, m)
            acc = jnp.zeros((self.groups, self.segs, self.seg, D), F32)
            for other in range(self.inner):
                if other != m:
                    reads = ((self.p ^ other) < (self.p ^ m)).astype(F32)
                    acc = acc + (w[:, (m ^ other).bit_length() - 1] * reads) * state[other][None]
            for bit, came in enumerate(outer):
                reads = ((self.outer >> bit) & 1).astype(F32)
                acc = acc + (w[:, self.inner_bits + bit] * reads) * came[None]
            back.append(acc.reshape(self.groups, self.rows, D))
        return [back[0]] + [exchange(back[m], "seq", m) for m in range(1, self.inner)], ext

    def backward(self, sends, ext):
        got = [sends[0]] + [exchange(sends[m], "seq", m) for m in range(1, self.inner)]
        grads = [x.reshape(self.groups, self.segs, self.seg, D) for x in got]
        weights = [self.take(ext, m) for m in range(self.inner)]

        def read_at(m, level):
            return jnp.sum(weights[m][:, level] * grads[m], axis=0)

        total = None
        for bit in reversed(range(self.bits - self.inner_bits)):
            reads = ((self.outer >> bit) & 1).astype(F32)
            send = reads * functools.reduce(
                lambda a, b: a + b, [read_at(m, self.inner_bits + bit) for m in range(self.inner)]
            )
            if total is not None:
                send = send + total
            came = exchange(send.reshape(self.rows, D), "seq", self.inner << bit).reshape(send.shape)
            total = came if total is None else total + came
        back = []
        for m in range(self.inner):
            acc = total if total is not None else jnp.zeros((self.segs, self.seg, D), F32)
            for other in range(self.inner):
                if other != m:
                    reads = ((self.p ^ other) > (self.p ^ m)).astype(F32)
                    acc = acc + reads * read_at(other, (m ^ other).bit_length() - 1)
            back.append(acc.reshape(self.rows, D))
        return [back[0]] + [exchange(back[m], "seq", m) for m in range(1, self.inner)]

    def gather_pieces(self, pieces):
        stacked = jnp.stack(pieces, 0)
        order = self.p ^ jnp.arange(self.inner)
        return jnp.moveaxis(jnp.take(stacked, order, axis=0), 0, -3).reshape(pieces[0].shape[:-2] + (self.inner * self.rows, D))

    def split_pieces(self, whole):
        parts = whole.reshape(whole.shape[:-2] + (self.inner, self.rows, D))
        return [lax.dynamic_index_in_dim(parts, self.p ^ m, parts.ndim - 3, keepdims=False) for m in range(self.inner)]


def local(query_rows, key_rows, value_rows, level_codes, norm_gain, upstream):
    tokens, width = query_rows.shape
    groups = tokens // GROUP
    heads = width // D
    features = width * lax.axis_size("head")
    chunks = tokens // CHUNK
    far = Far(groups, heads)
    first_far = log2(GROUP) + log2(groups) + 1
    pieces, each = (far.inner, heads // far.inner) if far.fast else (1, heads)
    pref = (far.p if far.fast else jnp.zeros_like(far.p)).astype(jnp.int32).reshape(1)
    gain = norm_gain.reshape(1, width)
    pair = 2 if heads % 2 == 0 else 1

    smem = pl.BlockSpec(memory_space=pltpu.SMEM)
    vmem = pl.BlockSpec(memory_space=pltpu.VMEM)
    wide = jax.ShapeDtypeStruct((tokens, width), F32)
    narrow = jax.ShapeDtypeStruct((tokens, width), BF16)
    tile16 = pltpu.VMEM((tokens, D), BF16)
    tile32 = pltpu.VMEM((tokens, D), F32)
    unit = tokens * D * D * heads

    def call(kernel, units, ins, outs, scratch=(), limit=12, **kw):
        kw.setdefault("out_specs", [vmem] * len(outs))
        return pl.pallas_call(
            kernel,
            in_specs=ins,
            out_shape=outs,
            scratch_shapes=list(scratch),
            compiler_params=pltpu.CompilerParams(vmem_limit_bytes=limit << 20),
            cost_estimate=pl.CostEstimate(flops=2 * units * unit, bytes_accessed=tokens * width * 8, transcendentals=0),
            **kw,
        )

    if far.fast:
        sends = call(
            functools.partial(state_kernel, pieces, each, (first_far, far.bits)),
            1,
            [smem, smem] + [pl.BlockSpec(memory_space=pltpu.HBM)] * 2,
            [jax.ShapeDtypeStruct((far.rows + far.extra, D), F32)] * pieces,
            [pltpu.VMEM((pieces, tokens, each * D), BF16)] * 2
            + [pltpu.VMEM((pieces, each * D, D), F32), pltpu.SemaphoreType.DMA((2, pieces))],
            limit=58,
        )(pref, level_codes, key_rows, value_rows)
    else:
        state = jnp.einsum(
            "she,shf->hef",
            key_rows.reshape(tokens, heads, D),
            value_rows.reshape(tokens, heads, D),
            preferred_element_type=F32,
        ).reshape(heads * D, D)
        lam = level_scale(level_codes)
        per_row = jnp.repeat(lam[:, first_far : first_far + far.bits, :], D // far.seg, axis=2)
        sends = []
        for m, piece in enumerate(far.split_pieces(state)):
            w = lax.dynamic_slice_in_dim(per_row, (far.p ^ m) * far.segs, far.segs, 2).reshape(-1, 1)
            w = jnp.pad(w, ((0, far.extra - w.shape[0]), (0, 0)))
            sends.append(jnp.concatenate([piece, jnp.broadcast_to(w, (far.extra, D))], 0))

    part, maps, att_t = call(
        functools.partial(inside_kernel, pair),
        5,
        [smem, vmem, vmem, vmem],
        [wide, jax.ShapeDtypeStruct((heads, chunks, D, D), BF16), narrow],
        [tile16] * pair,
    )(level_codes, query_rows, key_rows, value_rows)
    scaled = call(scale_kernel, 1, [vmem, vmem], [wide])(upstream, gain)[0]

    far_maps, ext = far.forward(sends)
    if not far.fast:
        far_maps = [far.gather_pieces(far_maps)]

    att, stats = call(
        functools.partial(attend_kernel, pieces, each),
        1,
        [smem] + [vmem] * (3 + pieces),
        [wide, jax.ShapeDtypeStruct((2, tokens), F32)],
        [pltpu.VMEM((heads, groups, D, D), BF16)],
    )(pref, query_rows, part, scaled, *far_maps)

    stats = sum_over(stats, "head")

    grad, *map_grads = call(
        functools.partial(grad_kernel, pieces, each, features),
        1,
        [smem] + [vmem] * 4,
        [narrow] + [jax.ShapeDtypeStruct((groups, each * D, D), F32)] * pieces,
        [tile32, tile32, pltpu.VMEM((heads, groups, D, D), F32)],
    )(pref, query_rows, att, scaled, stats)

    if not far.fast:
        map_grads = far.split_pieces(map_grads[0])

    query_gradient, normed = call(
        functools.partial(query_kernel, pieces, each, features),
        3,
        [smem, smem] + [vmem] * (7 + pieces),
        [narrow, narrow],
        [pltpu.VMEM((heads, groups, D, D), F32), tile32, tile16, tile32],
        grid=(heads,),
        out_specs=[pl.BlockSpec((tokens, D), lambda h: (0, h))] * 2,
    )(pref, level_codes, key_rows, value_rows, grad, maps, att, stats, gain, *far_maps)
    key_in, readers = call(
        key_kernel, 4, [smem] + [vmem] * 3, [wide, jax.ShapeDtypeStruct((heads, chunks, D, D), BF16)], [tile16, tile32]
    )(level_codes, query_rows, value_rows, grad)
    value_in = call(value_kernel, 2, [vmem] * 4, [wide])(key_rows, grad, att_t, readers)[0]

    state_grads = far.backward(map_grads, ext)
    if not far.fast:
        state_grads = [far.gather_pieces(state_grads)]

    key_gradient, value_gradient = call(
        functools.partial(outer_kernel, pieces, each),
        2,
        [smem] + [vmem] * (4 + pieces),
        [narrow, narrow],
        [pltpu.VMEM((heads, D, D), BF16)],
        grid=(tokens // CHUNK,),
        out_specs=[pl.BlockSpec((CHUNK, width), lambda i: (i, 0))] * 2,
    )(pref, key_rows, value_rows, key_in, value_in, *state_grads)
    return (normed, query_gradient, key_gradient, value_gradient)


def solution(mesh):
    return jax.shard_map(
        local,
        mesh=mesh,
        in_specs=(
            P("seq", "head"),
            P("seq", "head"),
            P("seq", "head"),
            P("seq", None, "head"),
            P("head"),
            P("seq", "head"),
        ),
        out_specs=(P("seq", "head"), P("seq", "head"), P("seq", "head"), P("seq", "head")),
        check_vma=False,
    )
```

```python
import functools
import math

import jax
import jax.numpy as jnp
from jax import lax
from jax.experimental import pallas as pl
from jax.experimental.pallas import tpu as pltpu
from jax.sharding import PartitionSpec as P


D = 128
GROUP = 1024
ROWS = 256
WIDE = 512
CHUNK = 128
F32 = jnp.float32
BF16 = jnp.bfloat16


def dot(a, b, ca, cb):
    return lax.dot_general(a, b, (((ca,), (cb,)), ((), ())), preferred_element_type=F32)


def level_scale(level_codes):
    levels = jnp.arange(level_codes.shape[1], dtype=F32)
    factor = jnp.where(levels > 0, jnp.exp2(-(levels - 1.0) * 0.5), 1.0) * 0.25
    return level_codes.astype(F32) * factor[None, :, None] * D ** (-0.5)


def log2(n):
    return n.bit_length() - 1


def weight(codes, g, level, h):
    factor = (2.0 ** (-(level - 1) / 2) if level else 1.0) / 4 / math.sqrt(D)
    return codes[g, h, level].astype(F32) * factor


def tile_weights(codes, g, h, transposed=False):
    rows = lax.broadcasted_iota(jnp.int32, (CHUNK, CHUNK), 0)
    cols = lax.broadcasted_iota(jnp.int32, (CHUNK, CHUNK), 1)
    apart = rows ^ cols
    w = jnp.full((CHUNK, CHUNK), weight(codes, g, 0, h), F32)
    for level in range(1, log2(CHUNK) + 1):
        w = jnp.where(apart >= (1 << (level - 1)), weight(codes, g, level, h), w)
    return jnp.where(rows <= cols if transposed else rows >= cols, w, 0.0)


def chunk_maps(states, codes, h, reverse=False):
    count = len(states)
    per_group = GROUP // CHUNK
    first = log2(CHUNK) + 1
    maps = [None] * count

    def add(a, b):
        return b if a is None else a + b

    if not reverse:
        blocks = list(states)
        for bit in range(log2(count)):
            for i in range(count):
                if (i >> bit) & 1:
                    maps[i] = add(maps[i], weight(codes, i // per_group, first + bit, h) * blocks[(i >> bit) ^ 1])
            blocks = [blocks[2 * a] + blocks[2 * a + 1] for a in range(len(blocks) // 2)]
    else:
        for bit in range(log2(count)):
            size = 1 << bit
            for block in range(1, count >> bit, 2):
                total = None
                for i in range(block * size, (block + 1) * size):
                    total = add(total, weight(codes, i // per_group, first + bit, h) * states[i])
                for i in range((block - 1) * size, block * size):
                    maps[i] = add(maps[i], total)
    return maps


def bf16_map(m):
    return jnp.zeros((D, D), BF16) if m is None else m.astype(BF16)


def chunk_rows(tokens):
    return [slice(i * CHUNK, (i + 1) * CHUNK) for i in range(tokens // CHUNK)]


def col(h):
    return pl.ds(pl.multiple_of(h * D, D), D)


def cat(a, b, axis):
    return jnp.concatenate([a, b], axis)


def add_states(state, first, k, v, r):
    for h in range(k.shape[1] // D):
        c = slice(h * D, (h + 1) * D)
        y = dot(k[r, c], v[r, c], 0, 0)
        state[h] = y if first else state[h] + y


def place(pieces):
    return lax.axis_index("seq") % pieces


def state_kernel(parts, each, far, codes_hbm, k_hbm, v_hbm, *refs):
    outs, (k, v, state, codes, sems, codes_sem) = refs[:parts], refs[parts:]
    blocks = [slice(i, i + ROWS) for i in range(0, k.shape[0], ROWS)]
    copies = []
    for n, r in enumerate(blocks):
        pair = [
            pltpu.make_async_copy(k_hbm.at[r, :], k.at[r, :], sems.at[0, n]),
            pltpu.make_async_copy(v_hbm.at[r, :], v.at[r, :], sems.at[1, n]),
        ]
        for c in pair:
            c.start()
        copies.append(pair)
        if n == 0:
            codes_copy = pltpu.make_async_copy(codes_hbm, codes, codes_sem)
            codes_copy.start()
    first, bits = far
    p = place(parts)
    index = lax.axis_index("seq")
    reads = [(lax.shift_right_logical(index, level) & 1).astype(F32) for level in range(bits)]
    codes_copy.wait()
    for m, out in enumerate(outs):
        row = each * D
        for level in range(bits):
            for i in range(each):
                w = weight(codes, 0, first + level, (m ^ p) * each + i)
                out[row : row + 1, :] = jnp.full((1, D), w * reads[level], F32)
                row += 1
        if row < out.shape[0]:
            out[row:, :] = jnp.zeros((out.shape[0] - row, D), F32)
    for n, r in enumerate(blocks):
        for c in copies[n]:
            c.wait()
        add_states(state, n == 0, k, v, r)
    for m, out in enumerate(outs):
        for i in range(each):
            out[i * D : (i + 1) * D, :] = state[(m ^ p) * each + i]


def inside_kernel(pair, codes, q, k, v, part, maps, att_t, *tiles):
    rows = chunk_rows(q.shape[0])
    per_group = GROUP // CHUNK

    @pl.loop(0, q.shape[1] // D // pair)
    def _(step):
        heads = [step * pair + n for n in range(pair)]
        for n, h in enumerate(heads):
            c = col(h)
            for i, r in enumerate(rows):
                if i % per_group == 0:
                    w = tile_weights(codes, i // per_group, h)
                tiles[n][r, :] = (w * dot(q[r, c], k[r, c], 1, 1)).astype(BF16)
            for i, r in enumerate(rows):
                if i % per_group == 0:
                    w = tile_weights(codes, i // per_group, h, transposed=True)
                att_t[r, c] = (w * dot(k[r, c], q[r, c], 1, 1)).astype(BF16)
            reads = chunk_maps([dot(k[r, c], v[r, c], 0, 0) for r in rows], codes, h)
            for i in range(len(rows)):
                maps[h, i] = bf16_map(reads[i])
        for n, h in enumerate(heads):
            c = col(h)
            for i, r in enumerate(rows):
                part[r, c] = dot(cat(tiles[n][r, :], q[r, c], 1), cat(v[r, c], maps[h, i], 0), 1, 0)


def scale_kernel(pieces, u, gain, scaled, zeros, spot):
    zeros[...] = jnp.zeros_like(zeros)
    spot[0] = place(pieces)

    @pl.loop(0, u.shape[0] // CHUNK)
    def _(i):
        r = pl.ds(pl.multiple_of(i * CHUNK, CHUNK), CHUNK)
        scaled[r, :] = u[r, :].astype(F32) * gain[...]


def sort_pieces(pieces, each, p, out):
    for m, piece in enumerate(pieces):
        for g in range(piece.shape[0]):
            for i in range(each):
                out[(m ^ p) * each + i, g] = piece[g, i * D : (i + 1) * D, :].astype(out.dtype)


def attend_kernel(offsets, pieces, each, q, part, scaled, stats_in, *refs):
    count = len(offsets)
    far, (att, stats, maps) = refs[:count], refs[count:]
    for n, piece in enumerate(far):
        for i in range(each):
            for g in range(piece.shape[0]):
                maps[n * each + i, g] = piece[g, i * D : (i + 1) * D, :].astype(BF16)

    def attend(heads):
        cols = [slice(h * D, (h + 1) * D) for h in heads]

        @pl.loop(0, q.shape[0] // WIDE)
        def _(step):
            r = pl.ds(pl.multiple_of(step * WIDE, WIDE), WIDE)
            g = (step * WIDE) // GROUP
            for n, c in enumerate(cols):
                att[r, c] = part[r, c] + dot(q[r, c], maps[n, g], 1, 0)
            for block in range(WIDE // CHUNK):
                b = pl.ds(pl.multiple_of(step * WIDE + block * CHUNK, CHUNK), CHUNK)
                squares = dots = None
                for n, c in enumerate(cols):
                    a = att[b, c]
                    squares = a * a if n == 0 else squares + a * a
                    dots = scaled[b, c] * a if n == 0 else dots + scaled[b, c] * a
                stats[0:1, b] = stats_in[0:1, b] + jnp.sum(squares.T, axis=0, keepdims=True)
                stats[1:2, b] = stats_in[1:2, b] + jnp.sum(dots.T, axis=0, keepdims=True)

    for p in range(pieces):

        @pl.when(place(pieces) == p)
        def _(p=p):
            attend([(m ^ p) * each + i for m in offsets for i in range(each)])


def token_factors(stats, features, inv_s, beta_s):
    @pl.loop(0, stats.shape[1] // CHUNK)
    def _(step):
        r = pl.ds(pl.multiple_of(step * CHUNK, CHUNK), CHUNK)
        inv = lax.rsqrt(stats[0:1, r] / features + 1e-06)
        inv_s[r, :] = jnp.broadcast_to(inv, (CHUNK, CHUNK)).T
        beta = inv * inv * inv * stats[1:2, r] / features
        beta_s[r, :] = jnp.broadcast_to(beta, (CHUNK, CHUNK)).T


def grad_kernel(pieces, each, features, q, att, scaled, stats, grad, *refs):
    outs, (inv, beta, sums) = refs[:pieces], refs[pieces:]
    token_factors(stats, features, inv, beta)
    groups = q.shape[0] // GROUP

    sums[...] = jnp.zeros_like(sums)

    @pl.loop(0, q.shape[0] // ROWS)
    def _(step):
        r = pl.ds(pl.multiple_of(step * ROWS, ROWS), ROWS)
        group = (step * ROWS) // GROUP
        for h in range(q.shape[1] // D):
            c = slice(h * D, (h + 1) * D)
            gr = (inv[r, :] * scaled[r, c] - att[r, c] * beta[r, :]).astype(BF16)
            grad[r, c] = gr
            sums[h, group] += dot(q[r, c], gr, 0, 0)

    for m, out in enumerate(outs):
        for g in range(groups):
            for i in range(each):
                out[g, i * D : (i + 1) * D, :] = sums[(m ^ place(pieces)) * each + i, g]


def query_kernel(pieces, each, codes, k, v, grad, maps, *refs):
    far, (dq, reach, tiles, outer) = refs[:pieces], refs[pieces:]
    h = pl.program_id(0)

    @pl.when(h == 0)
    def _():
        sort_pieces(far, each, place(pieces), reach)

    c = col(h)
    rows = chunk_rows(k.shape[0])
    per_group = GROUP // CHUNK
    for i, r in enumerate(rows):
        if i % per_group == 0:
            w = tile_weights(codes, i // per_group, h)
        to = (maps[h, i].astype(F32) + reach[h, i // per_group]).astype(BF16)
        y = dot(grad[r, c], cat(v[r, c], to, 0), 1, 1)
        tiles[r, :] = (w * y[:, :D]).astype(BF16)
        outer[r, :] = y[:, D:]
    for r in rows:
        dq[r, :] = (dot(tiles[r, :], k[r, c], 1, 0) + outer[r, :]).astype(BF16)


def normed_kernel(features, att, stats, gain, normed):
    for n in range(ROWS // CHUNK):
        start = pl.program_id(0) * ROWS + n * CHUNK
        b = pl.ds(pl.multiple_of(start, CHUNK), CHUNK)
        inv = jnp.broadcast_to(lax.rsqrt(stats[0:1, b] / features + 1e-06), (CHUNK, CHUNK)).T
        for h in range(att.shape[1] // D):
            c = slice(h * D, (h + 1) * D)
            normed[n * CHUNK : (n + 1) * CHUNK, c] = (att[b, c] * inv * gain[:, c]).astype(BF16)


def key_kernel(codes, q, v, grad, key_in, readers, tiles, outer):
    rows = chunk_rows(q.shape[0])
    per_group = GROUP // CHUNK

    @pl.loop(0, q.shape[1] // D)
    def _(h):
        c = col(h)
        sums = chunk_maps([dot(q[r, c], grad[r, c], 0, 0) for r in rows], codes, h, reverse=True)
        for i in range(len(rows)):
            readers[h, i] = bf16_map(sums[i])
        for i, r in enumerate(rows):
            if i % per_group == 0:
                w = tile_weights(codes, i // per_group, h, transposed=True)
            y = dot(v[r, c], cat(grad[r, c], readers[h, i], 0), 1, 1)
            tiles[r, :] = (w * y[:, :D]).astype(BF16)
            outer[r, :] = y[:, D:]
        for r in rows:
            key_in[r, c] = dot(tiles[r, :], q[r, c], 1, 0) + outer[r, :]


def value_kernel(k, grad, att_t, readers, value_in):
    rows = chunk_rows(k.shape[0])

    @pl.loop(0, k.shape[1] // D)
    def _(h):
        c = col(h)
        for i, r in enumerate(rows):
            value_in[r, c] = dot(cat(att_t[r, c], k[r, c], 1), cat(grad[r, c], readers[h, i], 0), 1, 0)


def outer_kernel(base, count, each, pref, k, v, key_in, value_in, *refs):
    far, (dk, dv, maps) = refs[:count], refs[-3:]
    j, step = pl.program_id(0), pl.program_id(1)

    @pl.when((j == 0) & (step == 0))
    def _():
        for n, piece in enumerate(far):
            for i in range(each):
                maps[n * each + i] = piece[i * D : (i + 1) * D, :].astype(BF16)

    r = pl.ds(pl.multiple_of(step * WIDE, WIDE), WIDE)
    for part in range(k.shape[1] // D // each):

        @pl.when((base + j) ^ pref[0] == part)
        def _(part=part):
            for i in range(each):
                c = slice((part * each + i) * D, (part * each + i + 1) * D)
                here = slice(i * D, (i + 1) * D)
                m = maps[j * each + i]
                dk[:, here] = (key_in[r, c] + dot(v[r, c], m, 1, 1)).astype(BF16)
                dv[:, here] = (value_in[r, c] + dot(k[r, c], m, 1, 0)).astype(BF16)


def exchange(x, axis, distance):
    count = lax.axis_size(axis)
    return lax.ppermute(x, axis, [(i, i ^ distance) for i in range(count)])


def sum_over(x, axis):
    count = lax.axis_size(axis)
    if count == 2:
        return x + exchange(x, axis, 1)
    return lax.psum(x, axis)


class Far:
    def __init__(self, groups, heads):
        self.count = lax.axis_size("seq")
        self.me = lax.axis_index("seq")
        self.inner = min(4, self.count)
        self.inner_bits = log2(self.inner)
        self.bits = log2(self.count)
        self.groups = groups
        self.rows = heads * D // self.inner
        self.seg = math.gcd(D, self.rows)
        self.segs = self.rows // self.seg
        used = groups * self.bits * self.segs
        self.extra = -(-used // 8) * 8
        self.p = self.me % self.inner
        self.fast = self.rows % D == 0 and groups == 1

    def take(self, ext, m):
        used = self.groups * self.bits * self.segs
        return ext[m][:used].reshape(self.groups, self.bits, self.segs, 1, D)

    def forward(self, sends):
        got = [sends[0]] + [exchange(sends[m], "seq", m) for m in range(1, self.inner)]
        state = [x[: self.rows].reshape(self.segs, self.seg, D) for x in got]
        ext = [x[self.rows :] for x in got]
        total = functools.reduce(lambda a, b: a + b, state)
        outer = []
        for bit in range(self.bits - self.inner_bits):
            came = exchange(total.reshape(self.rows, D), "seq", self.inner << bit).reshape(total.shape)
            outer.append(came)
            total = total + came
        back = []
        for m in range(self.inner):
            w = self.take(ext, m)
            acc = jnp.zeros((self.groups, self.segs, self.seg, D), F32)
            for other in range(self.inner):
                if other != m:
                    acc = acc + w[:, (m ^ other).bit_length() - 1] * state[other][None]
            for bit, came in enumerate(outer):
                acc = acc + w[:, self.inner_bits + bit] * came[None]
            back.append(acc.reshape(self.groups, self.rows, D))
        return [back[0]] + [exchange(back[m], "seq", m) for m in range(1, self.inner)], ext

    def backward(self, sends, ext):
        got = [sends[0]] + [exchange(sends[m], "seq", m) for m in range(1, self.inner)]
        grads = [x.reshape(self.groups, self.segs, self.seg, D) for x in got]
        weights = [self.take(ext, m) for m in range(self.inner)]

        def read_at(m, level):
            return jnp.sum(weights[m][:, level] * grads[m], axis=0)

        total = None
        for bit in reversed(range(self.bits - self.inner_bits)):
            send = functools.reduce(
                lambda a, b: a + b, [read_at(m, self.inner_bits + bit) for m in range(self.inner)]
            )
            if total is not None:
                send = send + total
            came = exchange(send.reshape(self.rows, D), "seq", self.inner << bit).reshape(send.shape)
            total = came if total is None else total + came
        back = []
        for m in range(self.inner):
            acc = total if total is not None else jnp.zeros((self.segs, self.seg, D), F32)
            for other in range(self.inner):
                if other != m:
                    acc = acc + read_at(other, (m ^ other).bit_length() - 1)
            back.append(acc.reshape(self.rows, D))
        return [back[0]] + [exchange(back[m], "seq", m) for m in range(1, self.inner)]

    def gather_pieces(self, pieces):
        stacked = jnp.stack(pieces, 0)
        order = self.p ^ jnp.arange(self.inner)
        return jnp.moveaxis(jnp.take(stacked, order, axis=0), 0, -3).reshape(pieces[0].shape[:-2] + (self.inner * self.rows, D))

    def split_pieces(self, whole):
        parts = whole.reshape(whole.shape[:-2] + (self.inner, self.rows, D))
        return [lax.dynamic_index_in_dim(parts, self.p ^ m, parts.ndim - 3, keepdims=False) for m in range(self.inner)]


def local(query_rows, key_rows, value_rows, level_codes, norm_gain, upstream):
    tokens, width = query_rows.shape
    groups = tokens // GROUP
    heads = width // D
    features = width * lax.axis_size("head")
    chunks = tokens // CHUNK
    far = Far(groups, heads)
    first_far = log2(GROUP) + log2(groups) + 1
    pieces, each = (far.inner, heads // far.inner) if far.fast else (1, heads)
    gain = norm_gain.reshape(1, width)
    codes = jnp.swapaxes(level_codes, 1, 2)
    pair = 2 if heads % 2 == 0 else 1

    smem = pl.BlockSpec(memory_space=pltpu.SMEM)
    vmem = pl.BlockSpec(memory_space=pltpu.VMEM)
    wide = jax.ShapeDtypeStruct((tokens, width), F32)
    narrow = jax.ShapeDtypeStruct((tokens, width), BF16)
    sums = jax.ShapeDtypeStruct((2, tokens), F32)
    turns = [(0, 1), (2, 3)] if pieces == 4 else [tuple(range(pieces))]
    tile16 = pltpu.VMEM((tokens, D), BF16)
    tile32 = pltpu.VMEM((tokens, D), F32)
    unit = tokens * D * D * heads

    def call(kernel, units, ins, outs, scratch=(), limit=12, **kw):
        if "grid_spec" not in kw:
            kw.setdefault("out_specs", [vmem] * len(outs))
            kw["in_specs"] = ins
            kw["scratch_shapes"] = list(scratch)
        return pl.pallas_call(
            kernel,
            out_shape=outs,
            compiler_params=pltpu.CompilerParams(vmem_limit_bytes=limit << 20),
            cost_estimate=pl.CostEstimate(flops=int(2 * units * unit), bytes_accessed=tokens * width * 8, transcendentals=0),
            **kw,
        )

    if far.fast:
        sends = call(
            functools.partial(state_kernel, pieces, each, (first_far, far.bits)),
            1,
            [pl.BlockSpec(memory_space=pltpu.HBM)] * 3,
            [jax.ShapeDtypeStruct((far.rows + far.extra, D), F32)] * pieces,
            [pltpu.VMEM((tokens, width), BF16)] * 2
            + [pltpu.VMEM((heads, D, D), F32), pltpu.SMEM(codes.shape, jnp.int32)]
            + [pltpu.SemaphoreType.DMA((2, tokens // ROWS)), pltpu.SemaphoreType.DMA],
            limit=58,
        )(codes, key_rows, value_rows)
        sends = list(sends)
    else:
        state = jnp.einsum(
            "she,shf->hef",
            key_rows.reshape(tokens, heads, D),
            value_rows.reshape(tokens, heads, D),
            preferred_element_type=F32,
        ).reshape(heads * D, D)
        lam = level_scale(level_codes)
        reads = (far.me >> jnp.arange(far.bits)) & 1
        weights = lam[:, first_far : first_far + far.bits, :] * reads.astype(F32)[None, :, None]
        per_row = jnp.repeat(weights, D // far.seg, axis=2)
        sends = []
        for m, piece in enumerate(far.split_pieces(state)):
            w = lax.dynamic_slice_in_dim(per_row, (far.p ^ m) * far.segs, far.segs, 2).reshape(-1, 1)
            w = jnp.pad(w, ((0, far.extra - w.shape[0]), (0, 0)))
            sends.append(jnp.concatenate([piece, jnp.broadcast_to(w, (far.extra, D))], 0))

    upstream, sends[1] = lax.optimization_barrier((upstream, sends[1]))
    part, maps, att_t = call(
        functools.partial(inside_kernel, pair),
        5,
        [smem, vmem, vmem, vmem],
        [wide, jax.ShapeDtypeStruct((heads, chunks, D, D), BF16), narrow],
        [tile16] * pair,
    )(codes, query_rows, key_rows, value_rows)
    scaled, stats, pref = call(
        functools.partial(scale_kernel, pieces),
        1,
        [vmem, vmem],
        [wide, sums, jax.ShapeDtypeStruct((1,), jnp.int32)],
        out_specs=[vmem, vmem, smem],
    )(upstream, gain)

    far_maps, ext = far.forward(sends)
    if not far.fast:
        far_maps = [far.gather_pieces(far_maps)]

    att = part
    for offsets in turns:
        att, stats = call(
            functools.partial(attend_kernel, offsets, pieces, each),
            1,
            [vmem] * (4 + len(offsets)),
            [wide, sums],
            [pltpu.VMEM((len(offsets) * each, groups, D, D), BF16)],
            input_output_aliases={1: 0},
        )(query_rows, att, scaled, stats, *[far_maps[m] for m in offsets])

    stats = sum_over(stats, "head")

    grad, *map_grads = call(
        functools.partial(grad_kernel, pieces, each, features),
        1,
        [vmem] * 4,
        [narrow] + [jax.ShapeDtypeStruct((groups, each * D, D), F32)] * pieces,
        [tile32, tile32, pltpu.VMEM((heads, groups, D, D), F32)],
    )(query_rows, att, scaled, stats)

    if not far.fast:
        map_grads = far.split_pieces(map_grads[0])

    query_gradient = call(
        functools.partial(query_kernel, pieces, each),
        3,
        [smem] + [vmem] * (4 + pieces),
        [narrow],
        [pltpu.VMEM((heads, groups, D, D), F32), tile16, tile32],
        grid=(heads,),
        out_specs=[pl.BlockSpec((tokens, D), lambda h: (0, h))],
    )(codes, key_rows, value_rows, grad, maps, *far_maps)[0]
    normed = call(
        functools.partial(normed_kernel, features),
        1,
        [vmem] * 3,
        [narrow],
        grid=(tokens // ROWS,),
        out_specs=[pl.BlockSpec((ROWS, width), lambda i: (i, 0))],
    )(att, stats, gain)[0]
    key_in, readers = call(
        key_kernel, 4, [smem] + [vmem] * 3, [wide, jax.ShapeDtypeStruct((heads, chunks, D, D), BF16)], [tile16, tile32]
    )(codes, query_rows, value_rows, grad)
    value_in = call(value_kernel, 2, [vmem] * 4, [wide])(key_rows, grad, att_t, readers)[0]

    state_grads = far.backward(map_grads, ext)
    if not far.fast:
        state_grads = [far.gather_pieces(state_grads)]

    done = []
    for offsets in turns:
        base, count = offsets[0], len(offsets)
        block = pl.BlockSpec((WIDE, each * D), lambda j, i, pref, base=base: (i, (base + j) ^ pref[0]))
        done = call(
            functools.partial(outer_kernel, base, count, each),
            2 / len(turns),
            None,
            [narrow, narrow],
            grid_spec=pltpu.PrefetchScalarGridSpec(
                num_scalar_prefetch=1,
                grid=(count, tokens // WIDE),
                in_specs=[vmem] * (4 + count) + [pl.BlockSpec(memory_space=pl.ANY)] * len(done),
                out_specs=[block, block],
                scratch_shapes=[pltpu.VMEM((count * each, D, D), BF16)],
            ),
            input_output_aliases={5 + count + i: i for i in range(len(done))},
        )(pref, key_rows, value_rows, key_in, value_in, *[state_grads[m] for m in offsets], *done)
    key_gradient, value_gradient = done
    return (normed, query_gradient, key_gradient, value_gradient)


def solution(mesh):
    return jax.shard_map(
        local,
        mesh=mesh,
        in_specs=(
            P("seq", "head"),
            P("seq", "head"),
            P("seq", "head"),
            P("seq", None, "head"),
            P("head"),
            P("seq", "head"),
        ),
        out_specs=(P("seq", "head"), P("seq", "head"), P("seq", "head"), P("seq", "head")),
        check_vma=False,
    )
```

```python
import functools
import math

import jax
import jax.numpy as jnp
from jax import lax
from jax.experimental import pallas as pl
from jax.experimental.pallas import tpu as pltpu
from jax.sharding import PartitionSpec as P


D = 128
GROUP = 1024
ROWS = 256
WIDE = 512
CHUNK = 128
F32 = jnp.float32
BF16 = jnp.bfloat16


def dot(a, b, ca, cb):
    return lax.dot_general(a, b, (((ca,), (cb,)), ((), ())), preferred_element_type=F32)


def level_scale(level_codes):
    levels = jnp.arange(level_codes.shape[1], dtype=F32)
    factor = jnp.where(levels > 0, jnp.exp2(-(levels - 1.0) * 0.5), 1.0) * 0.25
    return level_codes.astype(F32) * factor[None, :, None] * D ** (-0.5)


def log2(n):
    return n.bit_length() - 1


def weight(codes, g, level, h):
    factor = (2.0 ** (-(level - 1) / 2) if level else 1.0) / 4 / math.sqrt(D)
    return codes[g, h, level].astype(F32) * factor


def tile_weights(codes, g, h, transposed=False):
    rows = lax.broadcasted_iota(jnp.int32, (CHUNK, CHUNK), 0)
    cols = lax.broadcasted_iota(jnp.int32, (CHUNK, CHUNK), 1)
    apart = rows ^ cols
    w = jnp.full((CHUNK, CHUNK), weight(codes, g, 0, h), F32)
    for level in range(1, log2(CHUNK) + 1):
        w = jnp.where(apart >= (1 << (level - 1)), weight(codes, g, level, h), w)
    return jnp.where(rows <= cols if transposed else rows >= cols, w, 0.0)


def chunk_maps(states, codes, h, reverse=False):
    count = len(states)
    per_group = GROUP // CHUNK
    first = log2(CHUNK) + 1
    maps = [None] * count

    def add(a, b):
        return b if a is None else a + b

    if not reverse:
        blocks = list(states)
        for bit in range(log2(count)):
            for i in range(count):
                if (i >> bit) & 1:
                    maps[i] = add(maps[i], weight(codes, i // per_group, first + bit, h) * blocks[(i >> bit) ^ 1])
            blocks = [blocks[2 * a] + blocks[2 * a + 1] for a in range(len(blocks) // 2)]
    else:
        for bit in range(log2(count)):
            size = 1 << bit
            for block in range(1, count >> bit, 2):
                total = None
                for i in range(block * size, (block + 1) * size):
                    total = add(total, weight(codes, i // per_group, first + bit, h) * states[i])
                for i in range((block - 1) * size, block * size):
                    maps[i] = add(maps[i], total)
    return maps


def bf16_map(m):
    return jnp.zeros((D, D), BF16) if m is None else m.astype(BF16)


def chunk_rows(tokens):
    return [slice(i * CHUNK, (i + 1) * CHUNK) for i in range(tokens // CHUNK)]


def col(h):
    return pl.ds(pl.multiple_of(h * D, D), D)


def cat(a, b, axis):
    return jnp.concatenate([a, b], axis)


def add_states(state, first, k, v, r):
    for h in range(k.shape[1] // D):
        c = slice(h * D, (h + 1) * D)
        y = dot(k[r, c], v[r, c], 0, 0)
        state[h] = y if first else state[h] + y


def place(pieces):
    return lax.axis_index("seq") % pieces


def state_kernel(parts, each, far, codes_hbm, k_hbm, v_hbm, *refs):
    outs, (k, v, state, codes, sems, codes_sem) = refs[:parts], refs[parts:]
    blocks = [slice(i, i + ROWS) for i in range(0, k.shape[0], ROWS)]
    copies = []
    for n, r in enumerate(blocks):
        pair = [
            pltpu.make_async_copy(k_hbm.at[r, :], k.at[r, :], sems.at[0, n]),
            pltpu.make_async_copy(v_hbm.at[r, :], v.at[r, :], sems.at[1, n]),
        ]
        for c in pair:
            c.start()
        copies.append(pair)
        if n == 0:
            codes_copy = pltpu.make_async_copy(codes_hbm, codes, codes_sem)
            codes_copy.start()
    first, bits = far
    p = place(parts)
    index = lax.axis_index("seq")
    reads = [(lax.shift_right_logical(index, level) & 1).astype(F32) for level in range(bits)]
    codes_copy.wait()
    for m, out in enumerate(outs):
        row = each * D
        for level in range(bits):
            for i in range(each):
                w = weight(codes, 0, first + level, (m ^ p) * each + i)
                out[row : row + 1, :] = jnp.full((1, D), w * reads[level], F32)
                row += 1
        if row < out.shape[0]:
            out[row:, :] = jnp.zeros((out.shape[0] - row, D), F32)
    for n, r in enumerate(blocks):
        for c in copies[n]:
            c.wait()
        add_states(state, n == 0, k, v, r)
    for m, out in enumerate(outs):
        for i in range(each):
            out[i * D : (i + 1) * D, :] = state[(m ^ p) * each + i]


def inside_kernel(pair, codes, q, k, v, part, maps, att_t, *tiles):
    rows = chunk_rows(q.shape[0])
    per_group = GROUP // CHUNK

    @pl.loop(0, q.shape[1] // D // pair)
    def _(step):
        heads = [step * pair + n for n in range(pair)]
        for n, h in enumerate(heads):
            c = col(h)
            for i, r in enumerate(rows):
                if i % per_group == 0:
                    w = tile_weights(codes, i // per_group, h)
                tiles[n][r, :] = (w * dot(q[r, c], k[r, c], 1, 1)).astype(BF16)
            for i, r in enumerate(rows):
                if i % per_group == 0:
                    w = tile_weights(codes, i // per_group, h, transposed=True)
                att_t[r, c] = (w * dot(k[r, c], q[r, c], 1, 1)).astype(BF16)
            reads = chunk_maps([dot(k[r, c], v[r, c], 0, 0) for r in rows], codes, h)
            for i in range(len(rows)):
                maps[h, i] = bf16_map(reads[i])
        for n, h in enumerate(heads):
            c = col(h)
            for i, r in enumerate(rows):
                part[r, c] = dot(cat(tiles[n][r, :], q[r, c], 1), cat(v[r, c], maps[h, i], 0), 1, 0)


def scale_kernel(pieces, u, gain, send, scaled, zeros, spot, own):
    own[...] = send[...]
    zeros[...] = jnp.zeros_like(zeros)
    spot[0] = place(pieces)

    @pl.loop(0, u.shape[0] // CHUNK)
    def _(i):
        r = pl.ds(pl.multiple_of(i * CHUNK, CHUNK), CHUNK)
        scaled[r, :] = u[r, :].astype(F32) * gain[...]


def sort_pieces(pieces, each, p, out):
    for m, piece in enumerate(pieces):
        for g in range(piece.shape[0]):
            for i in range(each):
                out[(m ^ p) * each + i, g] = piece[g, i * D : (i + 1) * D, :].astype(out.dtype)


def attend_kernel(offsets, pieces, each, q, part, scaled, stats_in, *refs):
    count = len(offsets)
    far, (att, stats, maps) = refs[:count], refs[count:]
    for n, piece in enumerate(far):
        for i in range(each):
            for g in range(piece.shape[0]):
                maps[n * each + i, g] = piece[g, i * D : (i + 1) * D, :].astype(BF16)

    def attend(heads):
        cols = [slice(h * D, (h + 1) * D) for h in heads]

        @pl.loop(0, q.shape[0] // WIDE)
        def _(step):
            r = pl.ds(pl.multiple_of(step * WIDE, WIDE), WIDE)
            g = (step * WIDE) // GROUP
            for n, c in enumerate(cols):
                att[r, c] = part[r, c] + dot(q[r, c], maps[n, g], 1, 0)
            for block in range(WIDE // CHUNK):
                b = pl.ds(pl.multiple_of(step * WIDE + block * CHUNK, CHUNK), CHUNK)
                squares = dots = None
                for n, c in enumerate(cols):
                    a = att[b, c]
                    squares = a * a if n == 0 else squares + a * a
                    dots = scaled[b, c] * a if n == 0 else dots + scaled[b, c] * a
                stats[0:1, b] = stats_in[0:1, b] + jnp.sum(squares.T, axis=0, keepdims=True)
                stats[1:2, b] = stats_in[1:2, b] + jnp.sum(dots.T, axis=0, keepdims=True)

    for p in range(pieces):

        @pl.when(place(pieces) == p)
        def _(p=p):
            attend([(m ^ p) * each + i for m in offsets for i in range(each)])


def token_factors(stats, features, inv_s, beta_s):
    inv = lax.rsqrt(stats[0:1, :] / features + 1e-06)
    beta = inv * inv * inv * stats[1:2, :] / features
    both = jnp.concatenate([inv, beta, jnp.zeros((6, inv.shape[1]), F32)], 0)
    for r in chunk_rows(stats.shape[1]):
        turned = both[:, r].T
        inv_s[r, :] = jnp.broadcast_to(turned[:, 0:1], (CHUNK, CHUNK))
        beta_s[r, :] = jnp.broadcast_to(turned[:, 1:2], (CHUNK, CHUNK))


def grad_kernel(pieces, each, features, q, att, scaled, stats, grad, *refs):
    outs, (inv, beta, sums) = refs[:pieces], refs[pieces:]
    token_factors(stats, features, inv, beta)
    groups = q.shape[0] // GROUP

    for start in range(0, q.shape[0], ROWS):
        r = slice(start, start + ROWS)
        for h in range(q.shape[1] // D):
            c = slice(h * D, (h + 1) * D)
            gr = (inv[r, :] * scaled[r, c] - att[r, c] * beta[r, :]).astype(BF16)
            grad[r, c] = gr
            y = dot(q[r, c], gr, 0, 0)
            sums[h, start // GROUP] = y if start % GROUP == 0 else sums[h, start // GROUP] + y

    for m, out in enumerate(outs):
        for g in range(groups):
            for i in range(each):
                out[g, i * D : (i + 1) * D, :] = sums[(m ^ place(pieces)) * each + i, g]


def query_kernel(pieces, each, codes, k, v, grad, maps, *refs):
    far, (dq, reach, tiles, outer) = refs[:pieces], refs[pieces:]
    h = pl.program_id(0)

    @pl.when(h == 0)
    def _():
        sort_pieces(far, each, place(pieces), reach)

    c = col(h)
    rows = chunk_rows(k.shape[0])
    per_group = GROUP // CHUNK
    for i, r in enumerate(rows):
        if i % per_group == 0:
            w = tile_weights(codes, i // per_group, h)
        to = (maps[h, i].astype(F32) + reach[h, i // per_group]).astype(BF16)
        y = dot(grad[r, c], cat(v[r, c], to, 0), 1, 1)
        tiles[r, :] = (w * y[:, :D]).astype(BF16)
        outer[r, :] = y[:, D:]
    for r in rows:
        dq[r, :] = (dot(tiles[r, :], k[r, c], 1, 0) + outer[r, :]).astype(BF16)


def normed_kernel(features, att, stats, gain, normed):
    for n in range(WIDE // CHUNK):
        start = pl.program_id(0) * WIDE + n * CHUNK
        b = pl.ds(pl.multiple_of(start, CHUNK), CHUNK)
        inv = jnp.broadcast_to(lax.rsqrt(stats[0:1, b] / features + 1e-06), (CHUNK, CHUNK)).T
        for h in range(att.shape[1] // D):
            c = slice(h * D, (h + 1) * D)
            normed[n * CHUNK : (n + 1) * CHUNK, c] = (att[b, c] * inv * gain[:, c]).astype(BF16)


def key_kernel(codes, q, v, grad, key_in, readers, tiles, outer):
    rows = chunk_rows(q.shape[0])
    per_group = GROUP // CHUNK

    @pl.loop(0, q.shape[1] // D)
    def _(h):
        c = col(h)
        sums = chunk_maps([dot(q[r, c], grad[r, c], 0, 0) for r in rows], codes, h, reverse=True)
        for i in range(len(rows)):
            readers[h, i] = bf16_map(sums[i])
        for i, r in enumerate(rows):
            if i % per_group == 0:
                w = tile_weights(codes, i // per_group, h, transposed=True)
            y = dot(v[r, c], cat(grad[r, c], readers[h, i], 0), 1, 1)
            tiles[r, :] = (w * y[:, :D]).astype(BF16)
            outer[r, :] = y[:, D:]
        for r in rows:
            key_in[r, c] = dot(tiles[r, :], q[r, c], 1, 0) + outer[r, :]


def value_kernel(k, grad, att_t, readers, value_in):
    rows = chunk_rows(k.shape[0])

    @pl.loop(0, k.shape[1] // D)
    def _(h):
        c = col(h)
        for i, r in enumerate(rows):
            value_in[r, c] = dot(cat(att_t[r, c], k[r, c], 1), cat(grad[r, c], readers[h, i], 0), 1, 0)


def outer_kernel(base, count, each, pref, k, v, key_in, value_in, *refs):
    far, (dk, dv, maps) = refs[:count], refs[-3:]
    j = pl.program_id(0)

    @pl.when(j == 0)
    def _():
        for n, piece in enumerate(far):
            for i in range(each):
                maps[n * each + i] = piece[i * D : (i + 1) * D, :].astype(BF16)

    for part in range(k.shape[1] // D // each):

        @pl.when((base + j) ^ pref[0] == part)
        def _(part=part):
            for i in range(each):
                c = slice((part * each + i) * D, (part * each + i + 1) * D)
                here = slice(i * D, (i + 1) * D)
                m = maps[j * each + i]
                dk[:, here] = (key_in[:, c] + dot(v[:, c], m, 1, 1)).astype(BF16)
                dv[:, here] = (value_in[:, c] + dot(k[:, c], m, 1, 0)).astype(BF16)


def exchange(x, axis, distance):
    count = lax.axis_size(axis)
    return lax.ppermute(x, axis, [(i, i ^ distance) for i in range(count)])


def sum_over(x, axis):
    count = lax.axis_size(axis)
    if count == 2:
        return x + exchange(x, axis, 1)
    return lax.psum(x, axis)


class Far:
    def __init__(self, groups, heads):
        self.count = lax.axis_size("seq")
        self.me = lax.axis_index("seq")
        self.inner = min(4, self.count)
        self.inner_bits = log2(self.inner)
        self.bits = log2(self.count)
        self.groups = groups
        self.rows = heads * D // self.inner
        self.seg = math.gcd(D, self.rows)
        self.segs = self.rows // self.seg
        used = groups * self.bits * self.segs
        self.extra = -(-used // 8) * 8
        self.p = self.me % self.inner
        self.fast = self.rows % D == 0 and groups == 1

    def take(self, ext, m):
        used = self.groups * self.bits * self.segs
        return ext[m][:used].reshape(self.groups, self.bits, self.segs, 1, D)

    def forward(self, sends):
        got = [sends[0]] + [exchange(sends[m], "seq", m) for m in range(1, self.inner)]
        state = [x[: self.rows].reshape(self.segs, self.seg, D) for x in got]
        ext = [x[self.rows :] for x in got]
        total = functools.reduce(lambda a, b: a + b, state)
        outer = []
        for bit in range(self.bits - self.inner_bits):
            came = exchange(total.reshape(self.rows, D), "seq", self.inner << bit).reshape(total.shape)
            outer.append(came)
            total = total + came
        back = []
        for m in range(self.inner):
            w = self.take(ext, m)
            acc = jnp.zeros((self.groups, self.segs, self.seg, D), F32)
            for other in range(self.inner):
                if other != m:
                    acc = acc + w[:, (m ^ other).bit_length() - 1] * state[other][None]
            for bit, came in enumerate(outer):
                acc = acc + w[:, self.inner_bits + bit] * came[None]
            back.append(acc.reshape(self.groups, self.rows, D))
        return [back[0]] + [exchange(back[m], "seq", m) for m in range(1, self.inner)], ext

    def backward(self, sends, ext):
        got = [sends[0]] + [exchange(sends[m], "seq", m) for m in range(1, self.inner)]
        grads = [x.reshape(self.groups, self.segs, self.seg, D) for x in got]
        weights = [self.take(ext, m) for m in range(self.inner)]

        def read_at(m, level):
            return jnp.sum(weights[m][:, level] * grads[m], axis=0)

        total = None
        for bit in reversed(range(self.bits - self.inner_bits)):
            send = functools.reduce(
                lambda a, b: a + b, [read_at(m, self.inner_bits + bit) for m in range(self.inner)]
            )
            if total is not None:
                send = send + total
            came = exchange(send.reshape(self.rows, D), "seq", self.inner << bit).reshape(send.shape)
            total = came if total is None else total + came
        back = []
        for m in range(self.inner):
            acc = total if total is not None else jnp.zeros((self.segs, self.seg, D), F32)
            for other in range(self.inner):
                if other != m:
                    acc = acc + read_at(other, (m ^ other).bit_length() - 1)
            back.append(acc.reshape(self.rows, D))
        return [back[0]] + [exchange(back[m], "seq", m) for m in range(1, self.inner)]

    def gather_pieces(self, pieces):
        stacked = jnp.stack(pieces, 0)
        order = self.p ^ jnp.arange(self.inner)
        return jnp.moveaxis(jnp.take(stacked, order, axis=0), 0, -3).reshape(pieces[0].shape[:-2] + (self.inner * self.rows, D))

    def split_pieces(self, whole):
        parts = whole.reshape(whole.shape[:-2] + (self.inner, self.rows, D))
        return [lax.dynamic_index_in_dim(parts, self.p ^ m, parts.ndim - 3, keepdims=False) for m in range(self.inner)]


def local(query_rows, key_rows, value_rows, level_codes, norm_gain, upstream):
    tokens, width = query_rows.shape
    groups = tokens // GROUP
    heads = width // D
    features = width * lax.axis_size("head")
    chunks = tokens // CHUNK
    far = Far(groups, heads)
    first_far = log2(GROUP) + log2(groups) + 1
    pieces, each = (far.inner, heads // far.inner) if far.fast else (1, heads)
    gain = norm_gain.reshape(1, width)
    codes = jnp.swapaxes(level_codes, 1, 2)
    pair = 2 if heads % 2 == 0 else 1

    smem = pl.BlockSpec(memory_space=pltpu.SMEM)
    vmem = pl.BlockSpec(memory_space=pltpu.VMEM)
    wide = jax.ShapeDtypeStruct((tokens, width), F32)
    narrow = jax.ShapeDtypeStruct((tokens, width), BF16)
    sums = jax.ShapeDtypeStruct((2, tokens), F32)
    turns = [(0, 1), (2, 3)] if pieces == 4 else [tuple(range(pieces))]
    tile16 = pltpu.VMEM((tokens, D), BF16)
    tile32 = pltpu.VMEM((tokens, D), F32)
    unit = tokens * D * D * heads

    def call(kernel, units, ins, outs, scratch=(), limit=12, **kw):
        if "grid_spec" not in kw:
            kw.setdefault("out_specs", [vmem] * len(outs))
            kw["in_specs"] = ins
            kw["scratch_shapes"] = list(scratch)
        return pl.pallas_call(
            kernel,
            out_shape=outs,
            compiler_params=pltpu.CompilerParams(vmem_limit_bytes=limit << 20),
            cost_estimate=pl.CostEstimate(flops=int(2 * units * unit), bytes_accessed=tokens * width * 8, transcendentals=0),
            **kw,
        )

    if far.fast:
        sends = call(
            functools.partial(state_kernel, pieces, each, (first_far, far.bits)),
            1,
            [pl.BlockSpec(memory_space=pltpu.HBM)] * 3,
            [jax.ShapeDtypeStruct((far.rows + far.extra, D), F32)] * pieces,
            [pltpu.VMEM((tokens, width), BF16)] * 2
            + [pltpu.VMEM((heads, D, D), F32), pltpu.SMEM(codes.shape, jnp.int32)]
            + [pltpu.SemaphoreType.DMA((2, tokens // ROWS)), pltpu.SemaphoreType.DMA],
            limit=58,
        )(codes, key_rows, value_rows)
        sends = list(sends)
    else:
        state = jnp.einsum(
            "she,shf->hef",
            key_rows.reshape(tokens, heads, D),
            value_rows.reshape(tokens, heads, D),
            preferred_element_type=F32,
        ).reshape(heads * D, D)
        lam = level_scale(level_codes)
        reads = (far.me >> jnp.arange(far.bits)) & 1
        weights = lam[:, first_far : first_far + far.bits, :] * reads.astype(F32)[None, :, None]
        per_row = jnp.repeat(weights, D // far.seg, axis=2)
        sends = []
        for m, piece in enumerate(far.split_pieces(state)):
            w = lax.dynamic_slice_in_dim(per_row, (far.p ^ m) * far.segs, far.segs, 2).reshape(-1, 1)
            w = jnp.pad(w, ((0, far.extra - w.shape[0]), (0, 0)))
            sends.append(jnp.concatenate([piece, jnp.broadcast_to(w, (far.extra, D))], 0))

    upstream, sends[1] = lax.optimization_barrier((upstream, sends[1]))
    part, maps, att_t = call(
        functools.partial(inside_kernel, pair),
        5,
        [smem, vmem, vmem, vmem],
        [wide, jax.ShapeDtypeStruct((heads, chunks, D, D), BF16), narrow],
        [tile16] * pair,
    )(codes, query_rows, key_rows, value_rows)
    scaled, stats, pref, sends[0] = call(
        functools.partial(scale_kernel, pieces),
        1,
        [vmem] * 3,
        [wide, sums, jax.ShapeDtypeStruct((1,), jnp.int32), jax.ShapeDtypeStruct(sends[0].shape, F32)],
        out_specs=[vmem, vmem, smem, vmem],
    )(upstream, gain, sends[0])

    far_maps, ext = far.forward(sends)
    if not far.fast:
        far_maps = [far.gather_pieces(far_maps)]

    att = part
    for offsets in turns:
        att, stats = call(
            functools.partial(attend_kernel, offsets, pieces, each),
            1,
            [vmem] * (4 + len(offsets)),
            [wide, sums],
            [pltpu.VMEM((len(offsets) * each, groups, D, D), BF16)],
            input_output_aliases={1: 0},
        )(query_rows, att, scaled, stats, *[far_maps[m] for m in offsets])

    stats = sum_over(stats, "head")

    grad, *map_grads = call(
        functools.partial(grad_kernel, pieces, each, features),
        1,
        [vmem] * 4,
        [narrow] + [jax.ShapeDtypeStruct((groups, each * D, D), F32)] * pieces,
        [tile32, tile32, pltpu.VMEM((heads, groups, D, D), F32)],
    )(query_rows, att, scaled, stats)

    if not far.fast:
        map_grads = far.split_pieces(map_grads[0])

    query_gradient = call(
        functools.partial(query_kernel, pieces, each),
        3,
        [smem] + [vmem] * (4 + pieces),
        [narrow],
        [pltpu.VMEM((heads, groups, D, D), F32), tile16, tile32],
        grid=(heads,),
        out_specs=[pl.BlockSpec((tokens, D), lambda h: (0, h))],
    )(codes, key_rows, value_rows, grad, maps, *far_maps)[0]
    normed = call(
        functools.partial(normed_kernel, features),
        1,
        [vmem] * 3,
        [narrow],
        grid=(tokens // WIDE,),
        out_specs=[pl.BlockSpec((WIDE, width), lambda i: (i, 0))],
    )(att, stats, gain)[0]
    key_in, readers = call(
        key_kernel, 4, [smem] + [vmem] * 3, [wide, jax.ShapeDtypeStruct((heads, chunks, D, D), BF16)], [tile16, tile32]
    )(codes, query_rows, value_rows, grad)
    value_in = call(value_kernel, 2, [vmem] * 4, [wide])(key_rows, grad, att_t, readers)[0]

    state_grads = far.backward(map_grads, ext)
    if not far.fast:
        state_grads = [far.gather_pieces(state_grads)]

    done = []
    for offsets in turns:
        base, count = offsets[0], len(offsets)
        block = pl.BlockSpec((tokens, each * D), lambda j, pref, base=base: (0, (base + j) ^ pref[0]))
        done = call(
            functools.partial(outer_kernel, base, count, each),
            2 / len(turns),
            None,
            [narrow, narrow],
            grid_spec=pltpu.PrefetchScalarGridSpec(
                num_scalar_prefetch=1,
                grid=(count,),
                in_specs=[vmem] * (4 + count) + [pl.BlockSpec(memory_space=pl.ANY)] * len(done),
                out_specs=[block, block],
                scratch_shapes=[pltpu.VMEM((count * each, D, D), BF16)],
            ),
            input_output_aliases={5 + count + i: i for i in range(len(done))},
        )(pref, key_rows, value_rows, key_in, value_in, *[state_grads[m] for m in offsets], *done)
    key_gradient, value_gradient = done
    return (normed, query_gradient, key_gradient, value_gradient)


def solution(mesh):
    return jax.shard_map(
        local,
        mesh=mesh,
        in_specs=(
            P("seq", "head"),
            P("seq", "head"),
            P("seq", "head"),
            P("seq", None, "head"),
            P("head"),
            P("seq", "head"),
        ),
        out_specs=(P("seq", "head"), P("seq", "head"), P("seq", "head"), P("seq", "head")),
        check_vma=False,
    )
```

```python
import functools
import math

import jax
import jax.numpy as jnp
from jax import lax
from jax.experimental import pallas as pl
from jax.experimental.pallas import tpu as pltpu
from jax.sharding import PartitionSpec as P


D = 128
GROUP = 1024
ROWS = 256
WIDE = 512
CHUNK = 128
F32 = jnp.float32
BF16 = jnp.bfloat16


def dot(a, b, ca, cb):
    return lax.dot_general(a, b, (((ca,), (cb,)), ((), ())), preferred_element_type=F32)


def level_scale(level_codes):
    levels = jnp.arange(level_codes.shape[1], dtype=F32)
    factor = jnp.where(levels > 0, jnp.exp2(-(levels - 1.0) * 0.5), 1.0) * 0.25
    return level_codes.astype(F32) * factor[None, :, None] * D ** (-0.5)


def log2(n):
    return n.bit_length() - 1


def weight(codes, g, level, h):
    factor = (2.0 ** (-(level - 1) / 2) if level else 1.0) / 4 / math.sqrt(D)
    return codes[g, h, level].astype(F32) * factor


def tile_weights(codes, g, h, transposed=False):
    rows = lax.broadcasted_iota(jnp.int32, (CHUNK, CHUNK), 0)
    cols = lax.broadcasted_iota(jnp.int32, (CHUNK, CHUNK), 1)
    apart = rows ^ cols
    w = jnp.full((CHUNK, CHUNK), weight(codes, g, 0, h), F32)
    for level in range(1, log2(CHUNK) + 1):
        w = jnp.where(apart >= (1 << (level - 1)), weight(codes, g, level, h), w)
    return jnp.where(rows <= cols if transposed else rows >= cols, w, 0.0)


def chunk_maps(states, codes, h, reverse=False):
    count = len(states)
    per_group = GROUP // CHUNK
    first = log2(CHUNK) + 1
    maps = [None] * count

    def add(a, b):
        return b if a is None else a + b

    if not reverse:
        blocks = list(states)
        for bit in range(log2(count)):
            for i in range(count):
                if (i >> bit) & 1:
                    maps[i] = add(maps[i], weight(codes, i // per_group, first + bit, h) * blocks[(i >> bit) ^ 1])
            blocks = [blocks[2 * a] + blocks[2 * a + 1] for a in range(len(blocks) // 2)]
    else:
        for bit in range(log2(count)):
            size = 1 << bit
            for block in range(1, count >> bit, 2):
                total = None
                for i in range(block * size, (block + 1) * size):
                    total = add(total, weight(codes, i // per_group, first + bit, h) * states[i])
                for i in range((block - 1) * size, block * size):
                    maps[i] = add(maps[i], total)
    return maps


def bf16_map(m):
    return jnp.zeros((D, D), BF16) if m is None else m.astype(BF16)


def chunk_rows(tokens):
    return [slice(i * CHUNK, (i + 1) * CHUNK) for i in range(tokens // CHUNK)]


def col(h):
    return pl.ds(pl.multiple_of(h * D, D), D)


def cat(a, b, axis):
    return jnp.concatenate([a, b], axis)


def add_states(state, first, k, v, r):
    for h in range(k.shape[1] // D):
        c = slice(h * D, (h + 1) * D)
        y = dot(k[r, c], v[r, c], 0, 0)
        state[h] = y if first else state[h] + y


def place(pieces):
    return lax.axis_index("seq") % pieces


def state_kernel(parts, each, far, codes_hbm, k_hbm, v_hbm, *refs):
    outs, (k, v, state, codes, sems, codes_sem) = refs[:parts], refs[parts:]
    blocks = chunk_rows(k.shape[0])
    copies = []
    for n, r in enumerate(blocks):
        pair = [
            pltpu.make_async_copy(k_hbm.at[r, :], k.at[r, :], sems.at[0, n]),
            pltpu.make_async_copy(v_hbm.at[r, :], v.at[r, :], sems.at[1, n]),
        ]
        for c in pair:
            c.start()
        copies.append(pair)
        if n == 0:
            codes_copy = pltpu.make_async_copy(codes_hbm, codes, codes_sem)
            codes_copy.start()
    first, bits = far
    p = place(parts)
    index = lax.axis_index("seq")
    reads = [(lax.shift_right_logical(index, level) & 1).astype(F32) for level in range(bits)]
    codes_copy.wait()
    for m, out in enumerate(outs):
        row = each * D
        for level in range(bits):
            for i in range(each):
                w = weight(codes, 0, first + level, (m ^ p) * each + i)
                out[row : row + 1, :] = jnp.full((1, D), w * reads[level], F32)
                row += 1
        if row < out.shape[0]:
            out[row:, :] = jnp.zeros((out.shape[0] - row, D), F32)
    for n, r in enumerate(blocks):
        for c in copies[n]:
            c.wait()
        add_states(state, n == 0, k, v, r)
    for m, out in enumerate(outs):
        for i in range(each):
            out[i * D : (i + 1) * D, :] = state[(m ^ p) * each + i]


def inside_kernel(pair, codes, q, k, v, part, maps, att_t, *tiles):
    rows = chunk_rows(q.shape[0])
    per_group = GROUP // CHUNK

    @pl.loop(0, q.shape[1] // D // pair)
    def _(step):
        heads = [step * pair + n for n in range(pair)]
        for n, h in enumerate(heads):
            c = col(h)
            for i, r in enumerate(rows):
                if i % per_group == 0:
                    w = tile_weights(codes, i // per_group, h)
                tiles[n][r, :] = (w * dot(q[r, c], k[r, c], 1, 1)).astype(BF16)
            for i, r in enumerate(rows):
                if i % per_group == 0:
                    w = tile_weights(codes, i // per_group, h, transposed=True)
                att_t[r, c] = (w * dot(k[r, c], q[r, c], 1, 1)).astype(BF16)
            reads = chunk_maps([dot(k[r, c], v[r, c], 0, 0) for r in rows], codes, h)
            for i in range(len(rows)):
                maps[h, i] = bf16_map(reads[i])
        for n, h in enumerate(heads):
            c = col(h)
            for i, r in enumerate(rows):
                part[r, c] = dot(cat(tiles[n][r, :], q[r, c], 1), cat(v[r, c], maps[h, i], 0), 1, 0)


def scale_kernel(pieces, u, gain, send, scaled, zeros, spot, own):
    own[...] = send[...]
    zeros[...] = jnp.zeros_like(zeros)
    spot[0] = place(pieces)

    @pl.loop(0, u.shape[0] // CHUNK)
    def _(i):
        r = pl.ds(pl.multiple_of(i * CHUNK, CHUNK), CHUNK)
        scaled[r, :] = u[r, :].astype(F32) * gain[...]


def turn_kernel(q, turned):
    @pl.loop(0, q.shape[1] // D)
    def _(h):
        for r in chunk_rows(q.shape[0]):
            turned[col(h), r] = q[r, col(h)].T


def sort_pieces(pieces, each, p, out):
    for m, piece in enumerate(pieces):
        for g in range(piece.shape[0]):
            for i in range(each):
                out[(m ^ p) * each + i, g] = piece[g, i * D : (i + 1) * D, :].astype(out.dtype)


def attend_kernel(offsets, pieces, each, q, part, scaled, stats_in, *refs):
    count = len(offsets)
    far, (att, stats, maps) = refs[:count], refs[count:]
    for n, piece in enumerate(far):
        for i in range(each):
            for g in range(piece.shape[0]):
                maps[n * each + i, g] = piece[g, i * D : (i + 1) * D, :].astype(BF16)

    def attend(heads):
        cols = [slice(h * D, (h + 1) * D) for h in heads]

        @pl.loop(0, q.shape[0] // WIDE)
        def _(step):
            r = pl.ds(pl.multiple_of(step * WIDE, WIDE), WIDE)
            g = (step * WIDE) // GROUP
            for n, c in enumerate(cols):
                att[r, c] = part[r, c] + dot(q[r, c], maps[n, g], 1, 0)
            for block in range(WIDE // CHUNK):
                b = pl.ds(pl.multiple_of(step * WIDE + block * CHUNK, CHUNK), CHUNK)
                squares = dots = None
                for n, c in enumerate(cols):
                    a = att[b, c]
                    squares = a * a if n == 0 else squares + a * a
                    dots = scaled[b, c] * a if n == 0 else dots + scaled[b, c] * a
                stats[0:1, b] = stats_in[0:1, b] + jnp.sum(squares.T, axis=0, keepdims=True)
                stats[1:2, b] = stats_in[1:2, b] + jnp.sum(dots.T, axis=0, keepdims=True)

    for p in range(pieces):

        @pl.when(place(pieces) == p)
        def _(p=p):
            attend([(m ^ p) * each + i for m in offsets for i in range(each)])


def token_factors(stats, features, inv_s, beta_s):
    inv = lax.rsqrt(stats[0:1, :] / features + 1e-06)
    beta = inv * inv * inv * stats[1:2, :] / features
    both = jnp.concatenate([inv, beta, jnp.zeros((6, inv.shape[1]), F32)], 0)
    for r in chunk_rows(stats.shape[1]):
        turned = both[:, r].T
        inv_s[r, :] = jnp.broadcast_to(turned[:, 0:1], (CHUNK, CHUNK))
        beta_s[r, :] = jnp.broadcast_to(turned[:, 1:2], (CHUNK, CHUNK))


def grad_kernel(pieces, each, features, q_turned, att, scaled, stats, grad, *refs):
    outs, (inv, beta, sums) = refs[:pieces], refs[pieces:]
    token_factors(stats, features, inv, beta)
    groups = att.shape[0] // GROUP

    for start in range(0, att.shape[0], ROWS):
        r = slice(start, start + ROWS)
        for h in range(att.shape[1] // D):
            c = slice(h * D, (h + 1) * D)
            gr = (inv[r, :] * scaled[r, c] - att[r, c] * beta[r, :]).astype(BF16)
            grad[r, c] = gr
            y = dot(q_turned[c, r], gr, 1, 0)
            sums[h, start // GROUP] = y if start % GROUP == 0 else sums[h, start // GROUP] + y

    for m, out in enumerate(outs):
        for g in range(groups):
            for i in range(each):
                out[g, i * D : (i + 1) * D, :] = sums[(m ^ place(pieces)) * each + i, g]


def query_kernel(pair, pieces, each, codes, k, v, grad, maps, *refs):
    far, (dq, reach, tiles, outer) = refs[:pieces], refs[pieces:]

    @pl.when(pl.program_id(0) == 0)
    def _():
        sort_pieces(far, each, place(pieces), reach)

    rows = chunk_rows(k.shape[0])
    per_group = GROUP // CHUNK
    heads = [pl.program_id(0) * pair + n for n in range(pair)]
    for n, h in enumerate(heads):
        c = col(h)
        for i, r in enumerate(rows):
            if i % per_group == 0:
                w = tile_weights(codes, i // per_group, h)
            to = (maps[h, i].astype(F32) + reach[h, i // per_group]).astype(BF16)
            y = dot(grad[r, c], cat(v[r, c], to, 0), 1, 1)
            tiles[n, r, :] = (w * y[:, :D]).astype(BF16)
            outer[n, r, :] = y[:, D:]
    for n, h in enumerate(heads):
        c = col(h)
        for r in rows:
            dq[r, n * D : (n + 1) * D] = (dot(tiles[n, r, :], k[r, c], 1, 0) + outer[n, r, :]).astype(BF16)


def normed_kernel(features, att, stats, gain, normed):
    for n in range(WIDE // CHUNK):
        start = pl.program_id(0) * WIDE + n * CHUNK
        b = pl.ds(pl.multiple_of(start, CHUNK), CHUNK)
        inv = jnp.broadcast_to(lax.rsqrt(stats[0:1, b] / features + 1e-06), (CHUNK, CHUNK)).T
        for h in range(att.shape[1] // D):
            c = slice(h * D, (h + 1) * D)
            normed[n * CHUNK : (n + 1) * CHUNK, c] = (att[b, c] * inv * gain[:, c]).astype(BF16)


def key_kernel(pair, codes, q, v, grad, key_in, readers, tiles, outer):
    rows = chunk_rows(q.shape[0])
    per_group = GROUP // CHUNK

    @pl.loop(0, q.shape[1] // D // pair)
    def _(step):
        heads = [step * pair + n for n in range(pair)]
        for h in heads:
            c = col(h)
            sums = chunk_maps([dot(q[r, c], grad[r, c], 0, 0) for r in rows], codes, h, reverse=True)
            for i in range(len(rows)):
                readers[h, i] = bf16_map(sums[i])
        for n, h in enumerate(heads):
            c = col(h)
            for i, r in enumerate(rows):
                if i % per_group == 0:
                    w = tile_weights(codes, i // per_group, h, transposed=True)
                y = dot(v[r, c], cat(grad[r, c], readers[h, i], 0), 1, 1)
                tiles[n, r, :] = (w * y[:, :D]).astype(BF16)
                outer[n, r, :] = y[:, D:]
        for n, h in enumerate(heads):
            c = col(h)
            for r in rows:
                key_in[r, c] = dot(tiles[n, r, :], q[r, c], 1, 0) + outer[n, r, :]


def value_kernel(k, grad, att_t, readers, value_in):
    rows = chunk_rows(k.shape[0])

    @pl.loop(0, k.shape[1] // D)
    def _(h):
        c = col(h)
        for i, r in enumerate(rows):
            value_in[r, c] = dot(cat(att_t[r, c], k[r, c], 1), cat(grad[r, c], readers[h, i], 0), 1, 0)


def outer_kernel(base, count, each, pref, k, v, key_in, value_in, *refs):
    far, (dk, dv, maps) = refs[:count], refs[-3:]
    j = pl.program_id(0)

    @pl.when(j == 0)
    def _():
        for n, piece in enumerate(far):
            for i in range(each):
                maps[n * each + i] = piece[i * D : (i + 1) * D, :].astype(BF16)

    for part in range(k.shape[1] // D // each):

        @pl.when((base + j) ^ pref[0] == part)
        def _(part=part):
            for i in range(each):
                c = slice((part * each + i) * D, (part * each + i + 1) * D)
                here = slice(i * D, (i + 1) * D)
                m = maps[j * each + i]
                dk[:, here] = (key_in[:, c] + dot(v[:, c], m, 1, 1)).astype(BF16)
                dv[:, here] = (value_in[:, c] + dot(k[:, c], m, 1, 0)).astype(BF16)


def exchange(x, axis, distance):
    count = lax.axis_size(axis)
    return lax.ppermute(x, axis, [(i, i ^ distance) for i in range(count)])


def sum_over(x, axis):
    count = lax.axis_size(axis)
    if count == 2:
        return x + exchange(x, axis, 1)
    return lax.psum(x, axis)


class Far:
    def __init__(self, groups, heads):
        self.count = lax.axis_size("seq")
        self.me = lax.axis_index("seq")
        self.inner = min(4, self.count)
        self.inner_bits = log2(self.inner)
        self.bits = log2(self.count)
        self.groups = groups
        self.rows = heads * D // self.inner
        self.seg = math.gcd(D, self.rows)
        self.segs = self.rows // self.seg
        used = groups * self.bits * self.segs
        self.extra = -(-used // 8) * 8
        self.p = self.me % self.inner
        self.fast = self.rows % D == 0 and groups == 1

    def take(self, ext, m):
        used = self.groups * self.bits * self.segs
        return ext[m][:used].reshape(self.groups, self.bits, self.segs, 1, D)

    def forward(self, sends):
        got = [sends[0]] + [exchange(sends[m], "seq", m) for m in range(1, self.inner)]
        state = [x[: self.rows].reshape(self.segs, self.seg, D) for x in got]
        ext = [x[self.rows :] for x in got]
        total = functools.reduce(lambda a, b: a + b, state)
        outer = []
        for bit in range(self.bits - self.inner_bits):
            came = exchange(total.reshape(self.rows, D), "seq", self.inner << bit).reshape(total.shape)
            outer.append(came)
            total = total + came
        back = []
        for m in range(self.inner):
            w = self.take(ext, m)
            acc = jnp.zeros((self.groups, self.segs, self.seg, D), F32)
            for other in range(self.inner):
                if other != m:
                    acc = acc + w[:, (m ^ other).bit_length() - 1] * state[other][None]
            for bit, came in enumerate(outer):
                acc = acc + w[:, self.inner_bits + bit] * came[None]
            back.append(acc.reshape(self.groups, self.rows, D))
        return [back[0]] + [exchange(back[m], "seq", m) for m in range(1, self.inner)], ext

    def backward(self, sends, ext):
        got = [sends[0]] + [exchange(sends[m], "seq", m) for m in range(1, self.inner)]
        grads = [x.reshape(self.groups, self.segs, self.seg, D) for x in got]
        weights = [self.take(ext, m) for m in range(self.inner)]

        def read_at(m, level):
            return jnp.sum(weights[m][:, level] * grads[m], axis=0)

        total = None
        for bit in reversed(range(self.bits - self.inner_bits)):
            send = functools.reduce(
                lambda a, b: a + b, [read_at(m, self.inner_bits + bit) for m in range(self.inner)]
            )
            if total is not None:
                send = send + total
            came = exchange(send.reshape(self.rows, D), "seq", self.inner << bit).reshape(send.shape)
            total = came if total is None else total + came
        back = []
        for m in range(self.inner):
            acc = total if total is not None else jnp.zeros((self.segs, self.seg, D), F32)
            for other in range(self.inner):
                if other != m:
                    acc = acc + read_at(other, (m ^ other).bit_length() - 1)
            back.append(acc.reshape(self.rows, D))
        return [back[0]] + [exchange(back[m], "seq", m) for m in range(1, self.inner)]

    def gather_pieces(self, pieces):
        stacked = jnp.stack(pieces, 0)
        order = self.p ^ jnp.arange(self.inner)
        return jnp.moveaxis(jnp.take(stacked, order, axis=0), 0, -3).reshape(pieces[0].shape[:-2] + (self.inner * self.rows, D))

    def split_pieces(self, whole):
        parts = whole.reshape(whole.shape[:-2] + (self.inner, self.rows, D))
        return [lax.dynamic_index_in_dim(parts, self.p ^ m, parts.ndim - 3, keepdims=False) for m in range(self.inner)]


def local(query_rows, key_rows, value_rows, level_codes, norm_gain, upstream):
    tokens, width = query_rows.shape
    groups = tokens // GROUP
    heads = width // D
    features = width * lax.axis_size("head")
    chunks = tokens // CHUNK
    far = Far(groups, heads)
    first_far = log2(GROUP) + log2(groups) + 1
    pieces, each = (far.inner, heads // far.inner) if far.fast else (1, heads)
    gain = norm_gain.reshape(1, width)
    codes = jnp.swapaxes(level_codes, 1, 2)
    pair = 2 if heads % 2 == 0 else 1

    smem = pl.BlockSpec(memory_space=pltpu.SMEM)
    vmem = pl.BlockSpec(memory_space=pltpu.VMEM)
    wide = jax.ShapeDtypeStruct((tokens, width), F32)
    narrow = jax.ShapeDtypeStruct((tokens, width), BF16)
    sums = jax.ShapeDtypeStruct((2, tokens), F32)
    together = [tuple(range(pieces))]
    up_turns = [(0, 1), (2,), (3,)] if pieces == 4 else together
    down_turns = [(0,), (1,), (2, 3)] if pieces == 4 else together
    tile16 = pltpu.VMEM((tokens, D), BF16)
    tile32 = pltpu.VMEM((tokens, D), F32)
    tiles16 = pltpu.VMEM((pair, tokens, D), BF16)
    tiles32 = pltpu.VMEM((pair, tokens, D), F32)
    unit = tokens * D * D * heads

    def call(kernel, units, ins, outs, scratch=(), limit=12, **kw):
        if "grid_spec" not in kw:
            kw.setdefault("out_specs", [vmem] * len(outs))
            kw["in_specs"] = ins
            kw["scratch_shapes"] = list(scratch)
        return pl.pallas_call(
            kernel,
            out_shape=outs,
            compiler_params=pltpu.CompilerParams(vmem_limit_bytes=limit << 20),
            cost_estimate=pl.CostEstimate(flops=int(2 * units * unit), bytes_accessed=tokens * width * 8, transcendentals=0),
            **kw,
        )

    if far.fast:
        sends = call(
            functools.partial(state_kernel, pieces, each, (first_far, far.bits)),
            1,
            [pl.BlockSpec(memory_space=pltpu.HBM)] * 3,
            [jax.ShapeDtypeStruct((far.rows + far.extra, D), F32)] * pieces,
            [pltpu.VMEM((tokens, width), BF16)] * 2
            + [pltpu.VMEM((heads, D, D), F32), pltpu.SMEM(codes.shape, jnp.int32)]
            + [pltpu.SemaphoreType.DMA((2, tokens // CHUNK)), pltpu.SemaphoreType.DMA],
            limit=58,
        )(codes, key_rows, value_rows)
        sends = list(sends)
    else:
        state = jnp.einsum(
            "she,shf->hef",
            key_rows.reshape(tokens, heads, D),
            value_rows.reshape(tokens, heads, D),
            preferred_element_type=F32,
        ).reshape(heads * D, D)
        lam = level_scale(level_codes)
        reads = (far.me >> jnp.arange(far.bits)) & 1
        weights = lam[:, first_far : first_far + far.bits, :] * reads.astype(F32)[None, :, None]
        per_row = jnp.repeat(weights, D // far.seg, axis=2)
        sends = []
        for m, piece in enumerate(far.split_pieces(state)):
            w = lax.dynamic_slice_in_dim(per_row, (far.p ^ m) * far.segs, far.segs, 2).reshape(-1, 1)
            w = jnp.pad(w, ((0, far.extra - w.shape[0]), (0, 0)))
            sends.append(jnp.concatenate([piece, jnp.broadcast_to(w, (far.extra, D))], 0))

    upstream, sends[1] = lax.optimization_barrier((upstream, sends[1]))
    q_turned = call(turn_kernel, 1, [vmem], [jax.ShapeDtypeStruct((width, tokens), BF16)])(query_rows)[0]
    part, maps, att_t = call(
        functools.partial(inside_kernel, pair),
        5,
        [smem, vmem, vmem, vmem],
        [wide, jax.ShapeDtypeStruct((heads, chunks, D, D), BF16), narrow],
        [tile16] * pair,
    )(codes, query_rows, key_rows, value_rows)
    scaled, stats, pref, sends[0] = call(
        functools.partial(scale_kernel, pieces),
        1,
        [vmem] * 3,
        [wide, sums, jax.ShapeDtypeStruct((1,), jnp.int32), jax.ShapeDtypeStruct(sends[0].shape, F32)],
        out_specs=[vmem, vmem, smem, vmem],
    )(upstream, gain, sends[0])

    far_maps, ext = far.forward(sends)
    if not far.fast:
        far_maps = [far.gather_pieces(far_maps)]

    att = part
    for offsets in up_turns:
        att, stats = call(
            functools.partial(attend_kernel, offsets, pieces, each),
            1,
            [vmem] * (4 + len(offsets)),
            [wide, sums],
            [pltpu.VMEM((len(offsets) * each, groups, D, D), BF16)],
            input_output_aliases={1: 0},
        )(query_rows, att, scaled, stats, *[far_maps[m] for m in offsets])

    stats = sum_over(stats, "head")

    grad, *map_grads = call(
        functools.partial(grad_kernel, pieces, each, features),
        1,
        [vmem] * 4,
        [narrow] + [jax.ShapeDtypeStruct((groups, each * D, D), F32)] * pieces,
        [tile32, tile32, pltpu.VMEM((heads, groups, D, D), F32)],
    )(q_turned, att, scaled, stats)

    if not far.fast:
        map_grads = far.split_pieces(map_grads[0])

    query_gradient = call(
        functools.partial(query_kernel, pair, pieces, each),
        3,
        [smem] + [vmem] * (4 + pieces),
        [narrow],
        [pltpu.VMEM((heads, groups, D, D), F32), tiles16, tiles32],
        grid=(heads // pair,),
        out_specs=[pl.BlockSpec((tokens, pair * D), lambda h: (0, h))],
    )(codes, key_rows, value_rows, grad, maps, *far_maps)[0]
    normed = call(
        functools.partial(normed_kernel, features),
        1,
        [vmem] * 3,
        [narrow],
        grid=(tokens // WIDE,),
        out_specs=[pl.BlockSpec((WIDE, width), lambda i: (i, 0))],
    )(att, stats, gain)[0]
    key_in, readers = call(
        functools.partial(key_kernel, pair),
        4,
        [smem] + [vmem] * 3,
        [wide, jax.ShapeDtypeStruct((heads, chunks, D, D), BF16)],
        [tiles16, tiles32],
    )(codes, query_rows, value_rows, grad)
    value_in = call(value_kernel, 2, [vmem] * 4, [wide])(key_rows, grad, att_t, readers)[0]

    state_grads = far.backward(map_grads, ext)
    if not far.fast:
        state_grads = [far.gather_pieces(state_grads)]

    done = []
    for offsets in down_turns:
        base, count = offsets[0], len(offsets)
        block = pl.BlockSpec((tokens, each * D), lambda j, pref, base=base: (0, (base + j) ^ pref[0]))
        done = call(
            functools.partial(outer_kernel, base, count, each),
            2 / len(down_turns),
            None,
            [narrow, narrow],
            grid_spec=pltpu.PrefetchScalarGridSpec(
                num_scalar_prefetch=1,
                grid=(count,),
                in_specs=[vmem] * (4 + count) + [pl.BlockSpec(memory_space=pl.ANY)] * len(done),
                out_specs=[block, block],
                scratch_shapes=[pltpu.VMEM((count * each, D, D), BF16)],
            ),
            input_output_aliases={5 + count + i: i for i in range(len(done))},
        )(pref, key_rows, value_rows, key_in, value_in, *[state_grads[m] for m in offsets], *done)
    key_gradient, value_gradient = done
    return (normed, query_gradient, key_gradient, value_gradient)


def solution(mesh):
    return jax.shard_map(
        local,
        mesh=mesh,
        in_specs=(
            P("seq", "head"),
            P("seq", "head"),
            P("seq", "head"),
            P("seq", None, "head"),
            P("head"),
            P("seq", "head"),
        ),
        out_specs=(P("seq", "head"), P("seq", "head"), P("seq", "head"), P("seq", "head")),
        check_vma=False,
    )
```

```python
import functools
import math

import jax
import jax.numpy as jnp
from jax import lax
from jax.experimental import pallas as pl
from jax.experimental.pallas import tpu as pltpu
from jax.sharding import PartitionSpec as P


D = 128
GROUP = 1024
ROWS = 256
WIDE = 512
CHUNK = 128
F32 = jnp.float32
BF16 = jnp.bfloat16


def dot(a, b, ca, cb):
    return lax.dot_general(a, b, (((ca,), (cb,)), ((), ())), preferred_element_type=F32)


def level_scale(level_codes):
    levels = jnp.arange(level_codes.shape[1], dtype=F32)
    factor = jnp.where(levels > 0, jnp.exp2(-(levels - 1.0) * 0.5), 1.0) * 0.25
    return level_codes.astype(F32) * factor[None, :, None] * D ** (-0.5)


def log2(n):
    return n.bit_length() - 1


def weight(codes, g, level, h):
    factor = (2.0 ** (-(level - 1) / 2) if level else 1.0) / 4 / math.sqrt(D)
    return codes[g, h, level].astype(F32) * factor


def tile_weights(codes, g, h, transposed=False):
    rows = lax.broadcasted_iota(jnp.int32, (CHUNK, CHUNK), 0)
    cols = lax.broadcasted_iota(jnp.int32, (CHUNK, CHUNK), 1)
    apart = rows ^ cols
    w = jnp.full((CHUNK, CHUNK), weight(codes, g, 0, h), F32)
    for level in range(1, log2(CHUNK) + 1):
        w = jnp.where(apart >= (1 << (level - 1)), weight(codes, g, level, h), w)
    return jnp.where(rows <= cols if transposed else rows >= cols, w, 0.0)


def chunk_maps(states, codes, h, reverse=False):
    count = len(states)
    per_group = GROUP // CHUNK
    first = log2(CHUNK) + 1
    maps = [None] * count

    def add(a, b):
        return b if a is None else a + b

    if not reverse:
        blocks = list(states)
        for bit in range(log2(count)):
            for i in range(count):
                if (i >> bit) & 1:
                    maps[i] = add(maps[i], weight(codes, i // per_group, first + bit, h) * blocks[(i >> bit) ^ 1])
            blocks = [blocks[2 * a] + blocks[2 * a + 1] for a in range(len(blocks) // 2)]
    else:
        for bit in range(log2(count)):
            size = 1 << bit
            for block in range(1, count >> bit, 2):
                total = None
                for i in range(block * size, (block + 1) * size):
                    total = add(total, weight(codes, i // per_group, first + bit, h) * states[i])
                for i in range((block - 1) * size, block * size):
                    maps[i] = add(maps[i], total)
    return maps


def bf16_map(m):
    return jnp.zeros((D, D), BF16) if m is None else m.astype(BF16)


def chunk_rows(tokens):
    return [slice(i * CHUNK, (i + 1) * CHUNK) for i in range(tokens // CHUNK)]


def col(h):
    return pl.ds(pl.multiple_of(h * D, D), D)


def cat(a, b, axis):
    return jnp.concatenate([a, b], axis)


def add_states(state, first, k, v, r):
    for h in range(k.shape[1] // D):
        c = slice(h * D, (h + 1) * D)
        y = dot(k[r, c], v[r, c], 0, 0)
        state[h] = y if first else state[h] + y


def place(pieces):
    return lax.axis_index("seq") % pieces


def state_kernel(parts, each, far, codes_hbm, k_hbm, v_hbm, *refs):
    outs, (k, v, state, codes, sems, codes_sem) = refs[:parts], refs[parts:]
    blocks = chunk_rows(k.shape[0])
    copies = []
    for n, r in enumerate(blocks):
        pair = [
            pltpu.make_async_copy(k_hbm.at[r, :], k.at[r, :], sems.at[0, n]),
            pltpu.make_async_copy(v_hbm.at[r, :], v.at[r, :], sems.at[1, n]),
        ]
        for c in pair:
            c.start()
        copies.append(pair)
        if n == 0:
            codes_copy = pltpu.make_async_copy(codes_hbm, codes, codes_sem)
            codes_copy.start()
    first, bits = far
    p = place(parts)
    index = lax.axis_index("seq")
    reads = [(lax.shift_right_logical(index, level) & 1).astype(F32) for level in range(bits)]
    codes_copy.wait()
    for m, out in enumerate(outs):
        row = each * D
        for level in range(bits):
            for i in range(each):
                w = weight(codes, 0, first + level, (m ^ p) * each + i)
                out[row : row + 1, :] = jnp.full((1, D), w * reads[level], F32)
                row += 1
        if row < out.shape[0]:
            out[row:, :] = jnp.zeros((out.shape[0] - row, D), F32)
    for n, r in enumerate(blocks):
        for c in copies[n]:
            c.wait()
        add_states(state, n == 0, k, v, r)
    for m, out in enumerate(outs):
        for i in range(each):
            out[i * D : (i + 1) * D, :] = state[(m ^ p) * each + i]


def inside_kernel(pair, codes, q, k, v, part, maps, att_t, *tiles):
    rows = chunk_rows(q.shape[0])
    per_group = GROUP // CHUNK

    @pl.loop(0, q.shape[1] // D // pair)
    def _(step):
        heads = [step * pair + n for n in range(pair)]
        for n, h in enumerate(heads):
            c = col(h)
            for i, r in enumerate(rows):
                if i % per_group == 0:
                    w = tile_weights(codes, i // per_group, h)
                tiles[n][r, :] = (w * dot(q[r, c], k[r, c], 1, 1)).astype(BF16)
            for i, r in enumerate(rows):
                if i % per_group == 0:
                    w = tile_weights(codes, i // per_group, h, transposed=True)
                att_t[r, c] = (w * dot(k[r, c], q[r, c], 1, 1)).astype(BF16)
            reads = chunk_maps([dot(k[r, c], v[r, c], 0, 0) for r in rows], codes, h)
            for i in range(len(rows)):
                maps[h, i] = bf16_map(reads[i])
        for n, h in enumerate(heads):
            c = col(h)
            for i, r in enumerate(rows):
                part[r, c] = dot(cat(tiles[n][r, :], q[r, c], 1), cat(v[r, c], maps[h, i], 0), 1, 0)


def scale_kernel(pieces, u, gain, send, scaled, zeros, spot, own):
    own[...] = send[...]
    zeros[...] = jnp.zeros_like(zeros)
    spot[0] = place(pieces)

    @pl.loop(0, u.shape[0] // CHUNK)
    def _(i):
        r = pl.ds(pl.multiple_of(i * CHUNK, CHUNK), CHUNK)
        scaled[r, :] = u[r, :].astype(F32) * gain[...]


def turn_kernel(q, turned):
    @pl.loop(0, q.shape[1] // D)
    def _(h):
        for r in chunk_rows(q.shape[0]):
            turned[col(h), r] = q[r, col(h)].T


def sort_pieces(pieces, each, p, out):
    for m, piece in enumerate(pieces):
        for g in range(piece.shape[0]):
            for i in range(each):
                out[(m ^ p) * each + i, g] = piece[g, i * D : (i + 1) * D, :].astype(out.dtype)


def attend_kernel(offsets, pieces, each, q, part, scaled, stats_in, *refs):
    count = len(offsets)
    far, (att, stats, maps) = refs[:count], refs[count:]
    for n, piece in enumerate(far):
        for i in range(each):
            for g in range(piece.shape[0]):
                maps[n * each + i, g] = piece[g, i * D : (i + 1) * D, :].astype(BF16)

    def attend(heads):
        cols = [slice(h * D, (h + 1) * D) for h in heads]

        for start in range(0, q.shape[0], WIDE):
            r = slice(start, start + WIDE)
            for n, c in enumerate(cols):
                att[r, c] = part[r, c] + dot(q[r, c], maps[n, start // GROUP], 1, 0)
            for begin in range(start, start + WIDE, CHUNK):
                b = slice(begin, begin + CHUNK)
                squares = dots = None
                for n, c in enumerate(cols):
                    a = att[b, c]
                    squares = a * a if n == 0 else squares + a * a
                    dots = scaled[b, c] * a if n == 0 else dots + scaled[b, c] * a
                stats[0:1, b] = stats_in[0:1, b] + jnp.sum(squares.T, axis=0, keepdims=True)
                stats[1:2, b] = stats_in[1:2, b] + jnp.sum(dots.T, axis=0, keepdims=True)

    for p in range(pieces):

        @pl.when(place(pieces) == p)
        def _(p=p):
            attend([(m ^ p) * each + i for m in offsets for i in range(each)])


def token_factors(stats, features, inv_s, beta_s):
    inv = lax.rsqrt(stats[0:1, :] / features + 1e-06)
    beta = inv * inv * inv * stats[1:2, :] / features
    both = jnp.concatenate([inv, beta, jnp.zeros((6, inv.shape[1]), F32)], 0)
    for r in chunk_rows(stats.shape[1]):
        turned = both[:, r].T
        inv_s[r, :] = jnp.broadcast_to(turned[:, 0:1], (CHUNK, CHUNK))
        beta_s[r, :] = jnp.broadcast_to(turned[:, 1:2], (CHUNK, CHUNK))


def grad_kernel(pieces, each, features, q_turned, att, scaled, stats, grad, *refs):
    outs, (inv, beta, sums) = refs[:pieces], refs[pieces:]
    token_factors(stats, features, inv, beta)
    groups = att.shape[0] // GROUP

    for start in range(0, att.shape[0], ROWS):
        r = slice(start, start + ROWS)
        for h in range(att.shape[1] // D):
            c = slice(h * D, (h + 1) * D)
            gr = (inv[r, :] * scaled[r, c] - att[r, c] * beta[r, :]).astype(BF16)
            grad[r, c] = gr
            y = dot(q_turned[c, r], gr, 1, 0)
            sums[h, start // GROUP] = y if start % GROUP == 0 else sums[h, start // GROUP] + y

    for m, out in enumerate(outs):
        for g in range(groups):
            for i in range(each):
                out[g, i * D : (i + 1) * D, :] = sums[(m ^ place(pieces)) * each + i, g]


def query_kernel(pair, pieces, each, codes, k, v, grad, maps, *refs):
    far, (dq, reach, tiles, outer) = refs[:pieces], refs[pieces:]

    @pl.when(pl.program_id(0) == 0)
    def _():
        sort_pieces(far, each, place(pieces), reach)

    rows = chunk_rows(k.shape[0])
    per_group = GROUP // CHUNK
    heads = [pl.program_id(0) * pair + n for n in range(pair)]
    for n, h in enumerate(heads):
        c = col(h)
        for i, r in enumerate(rows):
            if i % per_group == 0:
                w = tile_weights(codes, i // per_group, h)
            to = (maps[h, i].astype(F32) + reach[h, i // per_group]).astype(BF16)
            y = dot(grad[r, c], cat(v[r, c], to, 0), 1, 1)
            tiles[n, r, :] = (w * y[:, :D]).astype(BF16)
            outer[n, r, :] = y[:, D:]
    for n, h in enumerate(heads):
        c = col(h)
        for r in rows:
            dq[r, n * D : (n + 1) * D] = (dot(tiles[n, r, :], k[r, c], 1, 0) + outer[n, r, :]).astype(BF16)


def normed_kernel(features, att, stats, gain, normed):
    for n in range(WIDE // CHUNK):
        start = pl.program_id(0) * WIDE + n * CHUNK
        b = pl.ds(pl.multiple_of(start, CHUNK), CHUNK)
        inv = jnp.broadcast_to(lax.rsqrt(stats[0:1, b] / features + 1e-06), (CHUNK, CHUNK)).T
        for h in range(att.shape[1] // D):
            c = slice(h * D, (h + 1) * D)
            normed[n * CHUNK : (n + 1) * CHUNK, c] = (att[b, c] * inv * gain[:, c]).astype(BF16)


def key_kernel(pair, codes, q, v, grad, key_in, readers, tiles, outer):
    rows = chunk_rows(q.shape[0])
    per_group = GROUP // CHUNK

    @pl.loop(0, q.shape[1] // D // pair)
    def _(step):
        heads = [step * pair + n for n in range(pair)]
        for h in heads:
            c = col(h)
            sums = chunk_maps([dot(q[r, c], grad[r, c], 0, 0) for r in rows], codes, h, reverse=True)
            for i in range(len(rows)):
                readers[h, i] = bf16_map(sums[i])
        for n, h in enumerate(heads):
            c = col(h)
            for i, r in enumerate(rows):
                if i % per_group == 0:
                    w = tile_weights(codes, i // per_group, h, transposed=True)
                y = dot(v[r, c], cat(grad[r, c], readers[h, i], 0), 1, 1)
                tiles[n, r, :] = (w * y[:, :D]).astype(BF16)
                outer[n, r, :] = y[:, D:]
        for n, h in enumerate(heads):
            c = col(h)
            for r in rows:
                key_in[r, c] = dot(tiles[n, r, :], q[r, c], 1, 0) + outer[n, r, :]


def value_kernel(k, grad, att_t, readers, value_in):
    rows = chunk_rows(k.shape[0])

    @pl.loop(0, k.shape[1] // D)
    def _(h):
        c = col(h)
        for i, r in enumerate(rows):
            value_in[r, c] = dot(cat(att_t[r, c], k[r, c], 1), cat(grad[r, c], readers[h, i], 0), 1, 0)


def outer_kernel(base, count, each, pref, k, v, key_in, value_in, *refs):
    far, (dk, dv, maps) = refs[:count], refs[-3:]
    j = pl.program_id(0)

    @pl.when(j == 0)
    def _():
        for n, piece in enumerate(far):
            for i in range(each):
                maps[n * each + i] = piece[i * D : (i + 1) * D, :].astype(BF16)

    for part in range(k.shape[1] // D // each):

        @pl.when((base + j) ^ pref[0] == part)
        def _(part=part):
            for i in range(each):
                c = slice((part * each + i) * D, (part * each + i + 1) * D)
                here = slice(i * D, (i + 1) * D)
                m = maps[j * each + i]
                dk[:, here] = (key_in[:, c] + dot(v[:, c], m, 1, 1)).astype(BF16)
                dv[:, here] = (value_in[:, c] + dot(k[:, c], m, 1, 0)).astype(BF16)


def exchange(x, axis, distance):
    count = lax.axis_size(axis)
    return lax.ppermute(x, axis, [(i, i ^ distance) for i in range(count)])


def sum_over(x, axis):
    count = lax.axis_size(axis)
    if count == 2:
        return x + exchange(x, axis, 1)
    return lax.psum(x, axis)


class Far:
    def __init__(self, groups, heads):
        self.count = lax.axis_size("seq")
        self.me = lax.axis_index("seq")
        self.inner = min(4, self.count)
        self.inner_bits = log2(self.inner)
        self.bits = log2(self.count)
        self.groups = groups
        self.rows = heads * D // self.inner
        self.seg = math.gcd(D, self.rows)
        self.segs = self.rows // self.seg
        used = groups * self.bits * self.segs
        self.extra = -(-used // 8) * 8
        self.p = self.me % self.inner
        self.fast = self.rows % D == 0 and groups == 1

    def take(self, ext, m):
        used = self.groups * self.bits * self.segs
        return ext[m][:used].reshape(self.groups, self.bits, self.segs, 1, D)

    def forward(self, sends):
        got = [sends[0]] + [exchange(sends[m], "seq", m) for m in range(1, self.inner)]
        state = [x[: self.rows].reshape(self.segs, self.seg, D) for x in got]
        ext = [x[self.rows :] for x in got]
        total = functools.reduce(lambda a, b: a + b, state)
        outer = []
        for bit in range(self.bits - self.inner_bits):
            came = exchange(total.reshape(self.rows, D), "seq", self.inner << bit).reshape(total.shape)
            outer.append(came)
            total = total + came
        back = []
        for m in range(self.inner):
            w = self.take(ext, m)
            acc = jnp.zeros((self.groups, self.segs, self.seg, D), F32)
            for other in range(self.inner):
                if other != m:
                    acc = acc + w[:, (m ^ other).bit_length() - 1] * state[other][None]
            for bit, came in enumerate(outer):
                acc = acc + w[:, self.inner_bits + bit] * came[None]
            back.append(acc.reshape(self.groups, self.rows, D))
        return [back[0]] + [exchange(back[m], "seq", m) for m in range(1, self.inner)], ext

    def backward(self, sends, ext):
        got = [sends[0]] + [exchange(sends[m], "seq", m) for m in range(1, self.inner)]
        grads = [x.reshape(self.groups, self.segs, self.seg, D) for x in got]
        weights = [self.take(ext, m) for m in range(self.inner)]

        def read_at(m, level):
            return jnp.sum(weights[m][:, level] * grads[m], axis=0)

        total = None
        for bit in reversed(range(self.bits - self.inner_bits)):
            send = functools.reduce(
                lambda a, b: a + b, [read_at(m, self.inner_bits + bit) for m in range(self.inner)]
            )
            if total is not None:
                send = send + total
            came = exchange(send.reshape(self.rows, D), "seq", self.inner << bit).reshape(send.shape)
            total = came if total is None else total + came
        back = []
        for m in range(self.inner):
            acc = total if total is not None else jnp.zeros((self.segs, self.seg, D), F32)
            for other in range(self.inner):
                if other != m:
                    acc = acc + read_at(other, (m ^ other).bit_length() - 1)
            back.append(acc.reshape(self.rows, D))
        return [back[0]] + [exchange(back[m], "seq", m) for m in range(1, self.inner)]

    def gather_pieces(self, pieces):
        stacked = jnp.stack(pieces, 0)
        order = self.p ^ jnp.arange(self.inner)
        return jnp.moveaxis(jnp.take(stacked, order, axis=0), 0, -3).reshape(pieces[0].shape[:-2] + (self.inner * self.rows, D))

    def split_pieces(self, whole):
        parts = whole.reshape(whole.shape[:-2] + (self.inner, self.rows, D))
        return [lax.dynamic_index_in_dim(parts, self.p ^ m, parts.ndim - 3, keepdims=False) for m in range(self.inner)]


def local(query_rows, key_rows, value_rows, level_codes, norm_gain, upstream):
    tokens, width = query_rows.shape
    groups = tokens // GROUP
    heads = width // D
    features = width * lax.axis_size("head")
    chunks = tokens // CHUNK
    far = Far(groups, heads)
    first_far = log2(GROUP) + log2(groups) + 1
    pieces, each = (far.inner, heads // far.inner) if far.fast else (1, heads)
    gain = norm_gain.reshape(1, width)
    codes = jnp.swapaxes(level_codes, 1, 2)
    pair = 2 if heads % 2 == 0 else 1

    smem = pl.BlockSpec(memory_space=pltpu.SMEM)
    vmem = pl.BlockSpec(memory_space=pltpu.VMEM)
    wide = jax.ShapeDtypeStruct((tokens, width), F32)
    narrow = jax.ShapeDtypeStruct((tokens, width), BF16)
    sums = jax.ShapeDtypeStruct((2, tokens), F32)
    together = [tuple(range(pieces))]
    up_turns = [(0, 1), (2,), (3,)] if pieces == 4 else together
    down_turns = [(0,), (1,), (2, 3)] if pieces == 4 else together
    tile16 = pltpu.VMEM((tokens, D), BF16)
    tile32 = pltpu.VMEM((tokens, D), F32)
    tiles16 = pltpu.VMEM((pair, tokens, D), BF16)
    tiles32 = pltpu.VMEM((pair, tokens, D), F32)
    unit = tokens * D * D * heads

    def call(kernel, units, ins, outs, scratch=(), limit=12, **kw):
        if "grid_spec" not in kw:
            kw.setdefault("out_specs", [vmem] * len(outs))
            kw["in_specs"] = ins
            kw["scratch_shapes"] = list(scratch)
        return pl.pallas_call(
            kernel,
            out_shape=outs,
            compiler_params=pltpu.CompilerParams(vmem_limit_bytes=limit << 20),
            cost_estimate=pl.CostEstimate(flops=int(2 * units * unit), bytes_accessed=tokens * width * 8, transcendentals=0),
            **kw,
        )

    if far.fast:
        sends = call(
            functools.partial(state_kernel, pieces, each, (first_far, far.bits)),
            1,
            [pl.BlockSpec(memory_space=pltpu.HBM)] * 3,
            [jax.ShapeDtypeStruct((far.rows + far.extra, D), F32)] * pieces,
            [pltpu.VMEM((tokens, width), BF16)] * 2
            + [pltpu.VMEM((heads, D, D), F32), pltpu.SMEM(codes.shape, jnp.int32)]
            + [pltpu.SemaphoreType.DMA((2, tokens // CHUNK)), pltpu.SemaphoreType.DMA],
            limit=58,
        )(codes, key_rows, value_rows)
        sends = list(sends)
    else:
        state = jnp.einsum(
            "she,shf->hef",
            key_rows.reshape(tokens, heads, D),
            value_rows.reshape(tokens, heads, D),
            preferred_element_type=F32,
        ).reshape(heads * D, D)
        lam = level_scale(level_codes)
        reads = (far.me >> jnp.arange(far.bits)) & 1
        weights = lam[:, first_far : first_far + far.bits, :] * reads.astype(F32)[None, :, None]
        per_row = jnp.repeat(weights, D // far.seg, axis=2)
        sends = []
        for m, piece in enumerate(far.split_pieces(state)):
            w = lax.dynamic_slice_in_dim(per_row, (far.p ^ m) * far.segs, far.segs, 2).reshape(-1, 1)
            w = jnp.pad(w, ((0, far.extra - w.shape[0]), (0, 0)))
            sends.append(jnp.concatenate([piece, jnp.broadcast_to(w, (far.extra, D))], 0))

    upstream, sends[1] = lax.optimization_barrier((upstream, sends[1]))
    q_turned = call(turn_kernel, 1, [vmem], [jax.ShapeDtypeStruct((width, tokens), BF16)])(query_rows)[0]
    part, maps, att_t = call(
        functools.partial(inside_kernel, pair),
        5,
        [smem, vmem, vmem, vmem],
        [wide, jax.ShapeDtypeStruct((heads, chunks, D, D), BF16), narrow],
        [tile16] * pair,
    )(codes, query_rows, key_rows, value_rows)
    scaled, stats, pref, sends[0] = call(
        functools.partial(scale_kernel, pieces),
        1,
        [vmem] * 3,
        [wide, sums, jax.ShapeDtypeStruct((1,), jnp.int32), jax.ShapeDtypeStruct(sends[0].shape, F32)],
        out_specs=[vmem, vmem, smem, vmem],
    )(upstream, gain, sends[0])

    far_maps, ext = far.forward(sends)
    if not far.fast:
        far_maps = [far.gather_pieces(far_maps)]

    att = part
    for offsets in up_turns:
        att, stats = call(
            functools.partial(attend_kernel, offsets, pieces, each),
            1,
            [vmem] * (4 + len(offsets)),
            [wide, sums],
            [pltpu.VMEM((len(offsets) * each, groups, D, D), BF16)],
            input_output_aliases={1: 0},
        )(query_rows, att, scaled, stats, *[far_maps[m] for m in offsets])

    stats = sum_over(stats, "head")

    grad, *map_grads = call(
        functools.partial(grad_kernel, pieces, each, features),
        1,
        [vmem] * 4,
        [narrow] + [jax.ShapeDtypeStruct((groups, each * D, D), F32)] * pieces,
        [tile32, tile32, pltpu.VMEM((heads, groups, D, D), F32)],
    )(q_turned, att, scaled, stats)

    if not far.fast:
        map_grads = far.split_pieces(map_grads[0])

    query_gradient = call(
        functools.partial(query_kernel, pair, pieces, each),
        3,
        [smem] + [vmem] * (4 + pieces),
        [narrow],
        [pltpu.VMEM((heads, groups, D, D), F32), tiles16, tiles32],
        grid=(heads // pair,),
        out_specs=[pl.BlockSpec((tokens, pair * D), lambda h: (0, h))],
    )(codes, key_rows, value_rows, grad, maps, *far_maps)[0]
    normed = call(
        functools.partial(normed_kernel, features),
        1,
        [vmem] * 3,
        [narrow],
        grid=(tokens // WIDE,),
        out_specs=[pl.BlockSpec((WIDE, width), lambda i: (i, 0))],
    )(att, stats, gain)[0]
    key_in, readers = call(
        functools.partial(key_kernel, pair),
        4,
        [smem] + [vmem] * 3,
        [wide, jax.ShapeDtypeStruct((heads, chunks, D, D), BF16)],
        [tiles16, tiles32],
    )(codes, query_rows, value_rows, grad)
    value_in = call(value_kernel, 2, [vmem] * 4, [wide])(key_rows, grad, att_t, readers)[0]

    state_grads = far.backward(map_grads, ext)
    if not far.fast:
        state_grads = [far.gather_pieces(state_grads)]

    done = []
    for offsets in down_turns:
        base, count = offsets[0], len(offsets)
        block = pl.BlockSpec((tokens, each * D), lambda j, pref, base=base: (0, (base + j) ^ pref[0]))
        done = call(
            functools.partial(outer_kernel, base, count, each),
            2 / len(down_turns),
            None,
            [narrow, narrow],
            grid_spec=pltpu.PrefetchScalarGridSpec(
                num_scalar_prefetch=1,
                grid=(count,),
                in_specs=[vmem] * (4 + count) + [pl.BlockSpec(memory_space=pl.ANY)] * len(done),
                out_specs=[block, block],
                scratch_shapes=[pltpu.VMEM((count * each, D, D), BF16)],
            ),
            input_output_aliases={5 + count + i: i for i in range(len(done))},
        )(pref, key_rows, value_rows, key_in, value_in, *[state_grads[m] for m in offsets], *done)
    key_gradient, value_gradient = done
    return (normed, query_gradient, key_gradient, value_gradient)


def solution(mesh):
    return jax.shard_map(
        local,
        mesh=mesh,
        in_specs=(
            P("seq", "head"),
            P("seq", "head"),
            P("seq", "head"),
            P("seq", None, "head"),
            P("head"),
            P("seq", "head"),
        ),
        out_specs=(P("seq", "head"), P("seq", "head"), P("seq", "head"), P("seq", "head")),
        check_vma=False,
    )
```
